1024 devices in a mesh: dp: 16 (over y, x_lo, core), seq: 64 (over x_hi, z).
Axes of the slice: x: 4 (x_hi: 2, x_lo: 2; x = x_hi * 2 + x_lo), y: 4, z: 32, core: 2. Of those that a mesh axis runs over, the one named last changes fastest.
Arguments:
- grad_out: bfloat16 [16, 8192, 4096], P('dp', 'seq'), may hold values from -6 to 6
- block_in: bfloat16 [16, 8192, 4096], P('dp', 'seq'), may hold values from -0.0234375 to 0.0234375
- residues: float32 [8, 4096], replicated, may hold values from -2 to 2
- decay_rates: float32 [8], replicated
Outputs:
- grad_in: bfloat16 [16, 8192, 4096], P('dp', 'seq')
- residue_grad: float32 [8, 4096], P(None, 'dp')
The draws below stay inside these ranges and needn't reach their ends.
All inputs are finite; a program needn't handle non-finite values.
Results may differ from the reference program's by a relative error of at most 0.0068.
Values sent between devices are 32-bit elements; how exact they have to be, the bound alone decides.
A program may use at most 64 MiB of HBM per device.

```python
import math
import jax
import jax.numpy as jnp
from jax import lax

C = 4096
MODES = 8
LDEV = 128
BATCH = 16
L_TOTAL = 8192


def draw_decay_rates(key, part):
    pick_key, slow_key, fast_key = jax.random.split(key, 3)
    slow_share = 0.625
    total_length = L_TOTAL * 1.0
    fast_lowest = min(8.0 / total_length, 1.0 / 60.0)
    chosen = jax.random.uniform(pick_key, (MODES,)) < slow_share
    slow_rates = jnp.exp(jax.random.uniform(slow_key, (MODES,), minval=math.log(0.2 / total_length), maxval=math.log(6.0 / total_length)))
    fast_rates = jnp.exp(jax.random.uniform(fast_key, (MODES,), minval=math.log(fast_lowest), maxval=math.log(1.0 / 30.0)))
    return jnp.where(chosen, slow_rates, fast_rates).astype(jnp.float32)


def draw_grad_out(key, part):
    noise_key = jax.random.fold_in(jax.random.fold_in(key, 7), 0)
    period_key = jax.random.fold_in(jax.random.fold_in(key, 7), 2)
    phase_key = jax.random.fold_in(jax.random.fold_in(key, 7), 3)
    shape = (BATCH, L_TOTAL, C)
    noise = jax.random.truncated_normal(noise_key, -5.0, 5.0, shape)
    period = LDEV * jnp.exp(jax.random.uniform(period_key, (1, 1, C), minval=math.log(0.98), maxval=math.log(1.02)))
    phase = jax.random.uniform(phase_key, (BATCH, 1, C), minval=-math.pi, maxval=math.pi)
    positions = jnp.arange(L_TOTAL, dtype=jnp.float32)[None, :, None]
    wave = 0.5 * jnp.sin(2.0 * math.pi * positions / period + phase)
    return (noise + wave).astype(jnp.bfloat16)


def raised(result, rng, source, target, parts, factor):
    def block_of(dim):
        return (jnp.arange(result.shape[dim]) // (result.shape[dim] // parts)).reshape((-1,) + (1,) * (result.ndim - 1 - dim))

    first = jax.random.permutation(rng, parts)[block_of(target)]
    second = (block_of(target) + parts // 2) % parts
    return jnp.where((block_of(source) == first) | (block_of(source) == second), factor * result, result)


def level_of(rng, extent, cuts, low, largest):
    level, own = 1.0, jax.random.fold_in(rng, 6)
    for dim, shards_of in cuts:
        draws = jnp.exp(jax.random.uniform(jax.random.fold_in(own, dim), (shards_of,), jnp.float32, low / len(cuts), largest / len(cuts)))
        level = level * jnp.repeat(draws, extent[dim] // shards_of).reshape([-1 if axis == dim else 1 for axis in range(len(extent))])
    return level


def normal_values(key, dims, scale, reach, cuts=(), kind=jnp.bfloat16):
    result = scale * jax.random.normal(key, dims, jnp.float32)
    if cuts:
        result = result * level_of(key, dims, cuts, -0.22, 0.18)
    return jnp.clip(result, -reach, reach).astype(kind)


def bell_draw_with(stream_key, shape, deviation, most, cuts, heavy, held_as=jnp.bfloat16):
    values = deviation * jax.random.normal(stream_key, shape, jnp.float32)
    if cuts:
        values = values * level_of(stream_key, shape, cuts, -0.22, 0.18)
    return jnp.clip(raised(values, jax.random.fold_in(stream_key, 3), *heavy), -most, most).astype(held_as)


def setup_inputs(seed: int = 0) -> dict:
    seeds = jax.random.split(jax.random.key(seed), 5)
    return {
        "grad_out": draw_grad_out(jax.random.fold_in(seeds[4], 71), 0),
        "block_in": bell_draw_with(seeds[1], (BATCH, L_TOTAL, C), (BATCH * L_TOTAL) ** -0.5, 0.0234375, ((0, 16), (1, 64)), (0, 2, 16, 2.0)),
        "residues": normal_values(seeds[2], (MODES, C), MODES ** -0.5, 2.0, (), jnp.float32),
        "decay_rates": draw_decay_rates(jax.random.fold_in(seeds[4], 71), 0),
    }


def modal_tables(decay_rates, block_rows):
    offsets = jnp.arange(block_rows, dtype=jnp.float32)
    mode_gain = jnp.sqrt(1.0 - jnp.exp(-2.0 * decay_rates))
    lag_steps = offsets[None, :] - offsets[:, None]
    decay_table = jnp.where(lag_steps[None] >= 0, mode_gain[:, None, None] * jnp.exp(-decay_rates[:, None, None] * jnp.maximum(lag_steps[None], 0.0)), 0.0).astype(jnp.bfloat16)
    carry_table = (mode_gain[None, :] * jnp.exp(-decay_rates[None, :] * (block_rows - offsets[:, None]))).astype(jnp.bfloat16)
    state_table = jnp.exp(-decay_rates[:, None] * offsets[None, :]).astype(jnp.bfloat16)
    block_decay = jnp.exp(-decay_rates * block_rows)
    return (decay_table, carry_table, state_table, block_decay)

def local_terms(grad_out, block_in, residues, decay_table, carry_table, state_table):
    batch_rows, block_rows, channel_count = grad_out.shape
    mode_count = residues.shape[0]
    stacked_table = jnp.transpose(decay_table, (1, 0, 2)).reshape(block_rows, mode_count * block_rows)
    scaled = (grad_out[:, None, :, :] * residues[None, :, None, :]).astype(jnp.bfloat16).reshape(batch_rows, mode_count * block_rows, channel_count)
    local_grad = jnp.einsum('sk,bkc->bsc', stacked_table, scaled, preferred_element_type=jnp.float32)
    block_state = jnp.einsum('rt,btc->brc', state_table, grad_out, preferred_element_type=jnp.float32)
    pieces = []
    for mode_index in range(mode_count):
        weighted = jnp.einsum('st,bsc->btc', decay_table[mode_index], block_in, preferred_element_type=jnp.float32)
        pieces.append(lax.optimization_barrier(jnp.sum(weighted * grad_out, axis=(0, 1))))
    local_part = jnp.stack(pieces)
    carry_weights = jnp.einsum('sr,bsc->brc', carry_table, block_in, preferred_element_type=jnp.float32)
    return (local_grad, block_state, local_part, carry_weights)

def reference(grad_out, block_in, residues, decay_rates):
    batch_rows, length, channel_count = grad_out.shape
    block_rows = LDEV
    block_count = length // block_rows
    mode_count = residues.shape[0]
    decay_table, carry_table, state_table, block_decay = modal_tables(decay_rates, block_rows)

    def blocks(array):
        return array.reshape(batch_rows, block_count, block_rows, channel_count).transpose(1, 0, 2, 3)

    def advance(incoming, pair):
        dy_block, in_block = pair
        local_grad, block_state, local_part, carry_weights = local_terms(dy_block, in_block, residues, decay_table, carry_table, state_table)
        carried = jnp.einsum('sr,brc->bsc', carry_table.astype(jnp.float32), residues[None] * incoming, precision=lax.Precision.HIGHEST)
        grad_block = (local_grad + carried).astype(jnp.bfloat16)
        part_sum = local_part + lax.optimization_barrier(jnp.sum(incoming * carry_weights, axis=0))
        following = block_state + block_decay[None, :, None] * incoming
        return (following, (grad_block, part_sum))
    start_state = jnp.zeros((batch_rows, mode_count, channel_count), jnp.float32)
    final_state, outputs = lax.scan(advance, start_state, (blocks(grad_out), blocks(block_in)), reverse=True)
    grad_blocks, part_sums = outputs
    grad_in = grad_blocks.transpose(1, 0, 2, 3).reshape(batch_rows, length, channel_count)
    return (grad_in, lax.optimization_barrier(jnp.sum(part_sums, axis=0)))
```

```python
import functools

import jax
import jax.numpy as jnp
from jax import lax
from jax.experimental import pallas as pl
from jax.experimental.pallas import tpu as pltpu
from jax.sharding import PartitionSpec as P

MESH = pl.DeviceIdType.MESH
F32 = jnp.float32
BF16 = jnp.bfloat16


def kernel(
    tiles, rates, g_hbm, x_hbm, res_hbm, gin_ref, rgrad_ref,
    g, x, res, dt, lg, s_out, w_out, l_out, s_in, w_in, l_in, inc_out, inc_in,
    tw_out, tw_in, x_out, x_in, lsum, lz_in, lr_out, lr_in, r_out, r_in,
    in_sem, snd, rcv, r_rcv,
):
    modes, rows = 8, 128
    d = lax.axis_index("dp")
    seq = lax.axis_index("seq")
    h, z = lax.div(seq, tiles), lax.rem(seq, tiles)
    p = 2 * d + h
    owner = lax.div(z, 2) == d

    def wrap(v):
        return lax.rem(v + tiles, tiles)

    def line(zz):
        return (d, h * tiles + zz)

    def plane(pp):
        return (lax.div(pp, 2), lax.rem(pp, 2) * tiles + z)

    def send(kind, src, dst, dev):
        pltpu.make_async_remote_copy(
            src_ref=src, dst_ref=dst, send_sem=snd.at[kind], recv_sem=rcv.at[kind],
            device_id=dev, device_id_type=MESH,
        ).start()

    def wait_tiles(buf, sem, lo, n):
        part = buf.at[pl.ds(lo, n)]
        pltpu.make_async_copy(part, part, sem).wait()

    copy_g = pltpu.make_async_copy(g_hbm.at[0], g, in_sem.at[0])
    copy_x = pltpu.make_async_copy(x_hbm.at[0], x, in_sem.at[1])
    copy_r = pltpu.make_async_copy(res_hbm, res, in_sem.at[2])
    copy_g.start()
    copy_x.start()
    copy_r.start()

    barrier = pltpu.get_barrier_semaphore()

    def greet(j, c):
        pl.semaphore_signal(barrier, inc=1, device_id=line(wrap(z + j)), device_id_type=MESH)
        pl.semaphore_signal(barrier, inc=1, device_id=plane(wrap(p + j)), device_id_type=MESH)
        return c

    lax.fori_loop(1, tiles, greet, 0)

    mode_row = lax.broadcasted_iota(jnp.int32, (modes, 128), 0)
    rate = jnp.zeros((modes, 128), F32)
    for r in range(modes):
        rate = jnp.where(mode_row == r, rates[r], rate)
    gain = jnp.sqrt(1.0 - jnp.exp(-2.0 * rate))
    pos = lax.broadcasted_iota(jnp.int32, (modes, 128), 1).astype(F32)
    state_table = jnp.exp(-rate * pos).astype(BF16)
    carry_t = (gain * jnp.exp(-rate * (rows - pos))).astype(BF16)
    decay = jnp.exp(-rate * float(rows))
    lag = (
        lax.broadcasted_iota(jnp.int32, (rows, rows), 1)
        - lax.broadcasted_iota(jnp.int32, (rows, rows), 0)
    ).astype(F32)
    causal = lag >= 0
    lag = jnp.maximum(lag, 0.0)
    for r in range(modes):
        full = jnp.full((rows, rows), rates[r], F32)
        gain_r = jnp.sqrt(1.0 - jnp.exp(-2.0 * full))
        dt[r] = jnp.where(causal, gain_r * jnp.exp(-full * lag), 0.0).astype(BF16)
    col = lax.rem(lax.broadcasted_iota(jnp.int32, (rows, 32), 1), modes)
    part = lax.div(lax.broadcasted_iota(jnp.int32, (rows, 32), 1), modes)
    at = lax.broadcasted_iota(jnp.int32, (rows, 32), 0).astype(F32)
    rate_c = jnp.zeros((rows, 32), F32)
    for r in range(modes):
        rate_c = jnp.where(col == r, rates[r], rate_c)
    gain_c = jnp.sqrt(1.0 - jnp.exp(-2.0 * rate_c))
    carry3 = jnp.where(part < 3, gain_c * jnp.exp(-rate_c * (rows - at)), 0.0).astype(BF16)

    copy_g.wait()
    copy_x.wait()
    copy_r.wait()

    def states(i, c):
        cols = pl.ds(pl.multiple_of(i * 256, 256), 256)
        s = jnp.dot(state_table, g[:, cols], preferred_element_type=F32)
        w = jnp.dot(carry_t, x[:, cols], preferred_element_type=F32)
        for t in range(2):
            s_out[2 * i + t] = s[:, t * 128:(t + 1) * 128]
            w_out[2 * i + t] = w[:, t * 128:(t + 1) * 128]
        return c

    lax.fori_loop(0, tiles // 2, states, 0)

    def local(i, c):
        cols = pl.ds(pl.multiple_of(i * 256, 256), 256)
        gc = g[:, cols]
        xc = x[:, cols].astype(F32)
        total = jnp.zeros((rows, 256), F32)
        sums = []
        for r in range(modes):
            v = jnp.dot(dt[r], gc, preferred_element_type=F32)
            total = total + v * res[r:r + 1, cols]
            sums.append(jnp.sum(v * xc, axis=0, keepdims=True))
        lg[:, cols] = total
        lp = jnp.concatenate(sums, axis=0)
        for t in range(2):
            l_out[2 * i + t] = lp[:, t * 128:(t + 1) * 128]
        return c

    lax.fori_loop(0, tiles // 2, local, 0)

    pl.semaphore_wait(barrier, 2 * (tiles - 1))

    S, W, LP, INC, TW, X, LZ, LR, R = range(9)

    def send_s(j, c):
        to = wrap(z + j)
        send(S, s_out.at[to], s_in.at[tiles - j], line(to))
        return c

    def send_w(j, c):
        to = wrap(z + j)
        send(W, w_out.at[to], w_in.at[tiles - j], line(to))
        return c

    def send_l(j, c):
        to = wrap(p + j)
        send(LP, l_out.at[to], l_in.at[tiles - j], plane(to))
        return c

    lax.fori_loop(1, tiles, send_s, 0)
    lax.fori_loop(1, tiles, send_w, 0)
    lax.fori_loop(1, tiles, send_l, 0)
    s_in[0] = s_out[z]
    w_in[0] = w_out[z]

    wait_tiles(l_in, rcv.at[LP], 1, tiles - 1)
    lsum[0] = l_out[p] + jnp.sum(l_in[1:tiles], axis=0)

    @pl.when(z != p)
    def _():
        send(LZ, lsum.at[0], lz_in.at[wrap(z - p)], line(p))

    wait_tiles(s_in, rcv.at[S], 1, tiles - 1)

    def scan(keep):
        def step(i, carry):
            slot = wrap(tiles - 1 - i - z)
            if keep:
                inc_out[slot] = carry
            return s_in[slot] + decay * carry
        return step

    tw_out[0] = lax.fori_loop(0, tiles, scan(False), jnp.zeros((modes, 128), F32), unroll=4)
    twin = plane(p + 1 - 2 * h)
    send(TW, tw_out.at[0], tw_in.at[0], twin)
    wait_tiles(tw_in, rcv.at[TW], 0, 1)
    start = jnp.where(h == 0, tw_in[0], 0.0)
    lax.fori_loop(0, tiles, scan(True), start, unroll=4)

    def send_inc(j, c):
        send(INC, inc_out.at[j], inc_in.at[tiles - j], line(wrap(z + j)))
        return c

    lax.fori_loop(1, tiles, send_inc, 0)
    inc_in[0] = inc_out[0]

    wait_tiles(w_in, rcv.at[W], 1, tiles - 1)
    cross = jnp.sum(inc_out[...] * w_in[...], axis=0)
    x_out[0] = cross
    to_d = 2 * lax.div(z, 2)
    for half in range(2):
        to = to_d + half

        @pl.when(to != p)
        def _(to=to):
            send(X, x_out.at[0], x_in.at[wrap(p - to)], plane(to))

    @pl.when(owner)
    def _():
        @pl.when(z == p)
        def _():
            wait_tiles(lz_in, rcv.at[LZ], 1, tiles - 1)
            lr_out[0] = lsum[0] + jnp.sum(lz_in[1:tiles], axis=0)
            send(LR, lr_out.at[0], lr_in.at[0], twin)

        @pl.when(z != p)
        def _():
            wait_tiles(lr_in, rcv.at[LR], 0, 1)
            lr_out[0] = lr_in[0]

        wait_tiles(x_in, rcv.at[X], 1, tiles - 1)
        r_out[0] = lr_out[0] + x_out[0] + jnp.sum(x_in[1:tiles], axis=0)

        def send_r(j, c):
            to = wrap(z + j)
            pltpu.make_async_remote_copy(
                src_ref=r_out.at[0], dst_ref=r_in.at[lax.rem(z, 2)],
                send_sem=snd.at[R], recv_sem=r_rcv.at[lax.rem(z, 2)],
                device_id=line(to), device_id_type=MESH,
            ).start()
            return c

        lax.fori_loop(1, tiles, send_r, 0)

    wait_tiles(inc_in, rcv.at[INC], 1, tiles - 1)

    def finish(i, c):
        cols = pl.ds(pl.multiple_of(i * 256, 256), 256)
        inc = jnp.concatenate([inc_in[wrap(2 * i - z)], inc_in[wrap(2 * i + 1 - z)]], axis=1)
        u = inc * res[:, cols]
        u0 = u.astype(BF16).astype(F32)
        u1 = (u - u0).astype(BF16).astype(F32)
        u2 = u - u0 - u1
        u3 = jnp.concatenate([u0, u1, u2, jnp.zeros_like(u)], axis=0).astype(BF16)
        out = lg[:, cols] + jnp.dot(carry3, u3, preferred_element_type=F32)
        gin_ref[0, :, cols] = out.astype(BF16)
        return c

    lax.fori_loop(0, tiles // 2, finish, 0)

    for i in range(2):
        mine = 2 * d + i == z

        @pl.when(jnp.logical_not(mine))
        def _(i=i):
            wait_tiles(r_in, r_rcv.at[i], i, 1)
            rgrad_ref[:, i * 128:(i + 1) * 128] = r_in[i]

        @pl.when(mine)
        def _(i=i):
            rgrad_ref[:, i * 128:(i + 1) * 128] = r_out[0]

    for kind, buf in ((S, s_in), (W, w_in), (LP, l_in), (INC, inc_in)):
        wait_tiles(buf, snd.at[kind], 1, tiles - 1)
    wait_tiles(tw_in, snd.at[TW], 0, 1)

    @pl.when(z != p)
    def _():
        wait_tiles(lsum, snd.at[LZ], 0, 1)

    for half in range(2):
        @pl.when(to_d + half != p)
        def _():
            wait_tiles(x_out, snd.at[X], 0, 1)

    @pl.when(owner)
    def _():
        wait_tiles(s_in, snd.at[R], 1, tiles - 1)

        @pl.when(z == p)
        def _():
            wait_tiles(lr_out, snd.at[LR], 0, 1)


def local(grad_out, block_in, residues, decay_rates):
    _, rows, channels = grad_out.shape
    tiles = channels // 128
    modes = residues.shape[0]
    vm = pltpu.VMEM
    many = vm((tiles, modes, 128), F32)
    one = vm((1, modes, 128), F32)
    anywhere = pl.BlockSpec(memory_space=pl.ANY)
    return pl.pallas_call(
        functools.partial(kernel, tiles),
        out_shape=(
            jax.ShapeDtypeStruct((1, rows, channels), BF16),
            jax.ShapeDtypeStruct((modes, 256), F32),
        ),
        in_specs=[pl.BlockSpec(memory_space=pltpu.SMEM), anywhere, anywhere, anywhere],
        out_specs=(pl.BlockSpec(memory_space=pltpu.VMEM), pl.BlockSpec(memory_space=pltpu.VMEM)),
        scratch_shapes=[
            vm((rows, channels), BF16),
            vm((rows, channels), BF16),
            vm((modes, channels), F32),
            vm((modes, rows, rows), BF16),
            vm((rows, channels), F32),
            many, many, many, many, many, many, many, many,
            one, one, one, many, one, many, one, one, one, vm((2, modes, 128), F32),
            pltpu.SemaphoreType.DMA((3,)),
            pltpu.SemaphoreType.DMA((9,)),
            pltpu.SemaphoreType.DMA((9,)),
            pltpu.SemaphoreType.DMA((2,)),
        ],
        compiler_params=pltpu.CompilerParams(collective_id=0, has_side_effects=True),
        name="modal_backward",
    )(decay_rates, grad_out, block_in, residues)


def solution(mesh):
    placed = (P("dp", "seq", None), P("dp", "seq", None), P(), P())
    return jax.shard_map(
        local,
        mesh=mesh,
        in_specs=placed,
        out_specs=(P("dp", "seq", None), P(None, "dp")),
        check_vma=False,
    )
```

```python
import functools

import jax
import jax.numpy as jnp
from jax import lax
from jax.experimental import pallas as pl
from jax.experimental.pallas import tpu as pltpu
from jax.sharding import PartitionSpec as P

MESH = pl.DeviceIdType.MESH
F32 = jnp.float32
BF16 = jnp.bfloat16


def kernel(
    tiles, rates, g_hbm, x_hbm, res_hbm, gin_ref, rgrad_ref,
    g, x, res, dt, lg, s_out, w_out, l_out, s_in, w_in, l_in, inc_out, inc_in,
    tw_out, tw_in, x_out, x_in, lsum, lz_in, r_out, r_in,
    in_sem, snd, rcv, r_rcv,
):
    modes, rows = 8, 128
    d = lax.axis_index("dp")
    seq = lax.axis_index("seq")
    h, z = lax.div(seq, tiles), lax.rem(seq, tiles)
    p = 2 * d + h
    owner = lax.div(z, 2) == d

    def wrap(v):
        return lax.rem(v + tiles, tiles)

    def line(zz):
        return (d, h * tiles + zz)

    def plane(pp):
        return (lax.div(pp, 2), lax.rem(pp, 2) * tiles + z)

    def send(kind, src, dst, dev):
        pltpu.make_async_remote_copy(
            src_ref=src, dst_ref=dst, send_sem=snd.at[kind], recv_sem=rcv.at[kind],
            device_id=dev, device_id_type=MESH,
        ).start()

    def wait_tiles(buf, sem, lo, n):
        part = buf.at[pl.ds(lo, n)]
        pltpu.make_async_copy(part, part, sem).wait()

    copy_g = pltpu.make_async_copy(g_hbm.at[0], g, in_sem.at[0])
    copy_x = pltpu.make_async_copy(x_hbm.at[0], x, in_sem.at[1])
    copy_r = pltpu.make_async_copy(res_hbm, res, in_sem.at[2])
    copy_g.start()
    copy_x.start()
    copy_r.start()

    barrier = pltpu.get_barrier_semaphore()

    def offset(i):
        m = lax.div(i, 2)
        return tiles // 2 + jnp.where(lax.rem(i, 2) == 0, m, -m)

    def greet_line(i, c):
        to = line(wrap(z + offset(i)))
        pl.semaphore_signal(barrier, inc=1, device_id=to, device_id_type=MESH)
        return c

    def greet_plane(j, c):
        to = plane(wrap(p + j))
        pl.semaphore_signal(barrier, inc=1, device_id=to, device_id_type=MESH)
        return c

    lax.fori_loop(1, tiles, greet_line, 0)
    lax.fori_loop(1, tiles, greet_plane, 0)

    mode_row = lax.broadcasted_iota(jnp.int32, (modes, 128), 0)
    rate = jnp.zeros((modes, 128), F32)
    for r in range(modes):
        rate = jnp.where(mode_row == r, rates[r], rate)
    gain = jnp.sqrt(1.0 - jnp.exp(-2.0 * rate))
    pos = lax.broadcasted_iota(jnp.int32, (modes, 128), 1).astype(F32)
    state_table = jnp.exp(-rate * pos).astype(BF16)
    carry_t = (gain * jnp.exp(-rate * (rows - pos))).astype(BF16)
    decay = jnp.exp(-rate * float(rows))
    lag = (
        lax.broadcasted_iota(jnp.int32, (rows, rows), 1)
        - lax.broadcasted_iota(jnp.int32, (rows, rows), 0)
    ).astype(F32)
    causal = lag >= 0
    lag = jnp.maximum(lag, 0.0)
    for r in range(modes):
        full = jnp.full((rows, rows), rates[r], F32)
        gain_r = jnp.sqrt(1.0 - jnp.exp(-2.0 * full))
        dt[r] = jnp.where(causal, gain_r * jnp.exp(-full * lag), 0.0).astype(BF16)
    col = lax.rem(lax.broadcasted_iota(jnp.int32, (rows, 32), 1), modes)
    part = lax.div(lax.broadcasted_iota(jnp.int32, (rows, 32), 1), modes)
    at = lax.broadcasted_iota(jnp.int32, (rows, 32), 0).astype(F32)
    rate_c = jnp.zeros((rows, 32), F32)
    for r in range(modes):
        rate_c = jnp.where(col == r, rates[r], rate_c)
    gain_c = jnp.sqrt(1.0 - jnp.exp(-2.0 * rate_c))
    carry3 = jnp.where(part < 3, gain_c * jnp.exp(-rate_c * (rows - at)), 0.0).astype(BF16)

    copy_g.wait()
    copy_x.wait()
    copy_r.wait()

    def states(i, c):
        cols = pl.ds(pl.multiple_of(i * 256, 256), 256)
        s = jnp.dot(state_table, g[:, cols], preferred_element_type=F32)
        w = jnp.dot(carry_t, x[:, cols], preferred_element_type=F32)
        for t in range(2):
            s_out[2 * i + t] = s[:, t * 128:(t + 1) * 128]
            w_out[2 * i + t] = w[:, t * 128:(t + 1) * 128]
        return c

    lax.fori_loop(0, tiles // 2, states, 0)

    def local(i, c):
        cols = pl.ds(pl.multiple_of(i * 256, 256), 256)
        gc = g[:, cols]
        xc = x[:, cols].astype(F32)
        total = jnp.zeros((rows, 256), F32)
        sums = []
        for r in range(modes):
            v = jnp.dot(dt[r], gc, preferred_element_type=F32)
            total = total + v * res[r:r + 1, cols]
            sums.append(jnp.sum(v * xc, axis=0, keepdims=True))
        lg[:, cols] = total
        lp = jnp.concatenate(sums, axis=0)
        for t in range(2):
            l_out[2 * i + t] = lp[:, t * 128:(t + 1) * 128]
        return c

    lax.fori_loop(0, tiles // 2, local, 0)

    pl.semaphore_wait(barrier, 2 * (tiles - 1))

    S, W, LP, INC, TW, X, LZ, R = range(8)

    def send_s(i, c):
        j = offset(i)
        to = wrap(z + j)
        send(S, s_out.at[to], s_in.at[tiles - j], line(to))
        return c

    def send_w(i, c):
        j = offset(i)
        to = wrap(z + j)
        send(W, w_out.at[to], w_in.at[tiles - j], line(to))
        return c

    def send_l(j, c):
        to = wrap(p + j)
        pair = pl.ds(2 * lax.div(to, 2), 2)
        send(LP, l_out.at[pair], l_in.at[tiles - j], plane(to))
        return c

    lax.fori_loop(1, tiles, send_l, 0)
    lax.fori_loop(1, tiles, send_s, 0)
    s_in[0] = s_out[z]
    w_in[0] = w_out[z]

    wait_tiles(l_in, rcv.at[LP], 1, tiles - 1)
    lsum[...] = l_out[pl.ds(2 * d, 2)] + jnp.sum(l_in[1:tiles], axis=0)
    for i in range(2):
        @pl.when(2 * d + i != z)
        def _(i=i):
            to = 2 * d + i
            send(LZ, lsum.at[i], lz_in.at[wrap(z - to)], line(to))

    lax.fori_loop(1, tiles, send_w, 0)

    wait_tiles(s_in, rcv.at[S], 1, tiles - 1)

    def scan(keep):
        def step(i, carry):
            slot = wrap(tiles - 1 - i - z)
            if keep:
                inc_out[slot] = carry
            return s_in[slot] + decay * carry
        return step

    tw_out[0] = lax.fori_loop(0, tiles, scan(False), jnp.zeros((modes, 128), F32), unroll=4)
    twin = plane(p + 1 - 2 * h)
    send(TW, tw_out.at[0], tw_in.at[0], twin)
    wait_tiles(tw_in, rcv.at[TW], 0, 1)
    start = jnp.where(h == 0, tw_in[0], 0.0)
    lax.fori_loop(0, tiles, scan(True), start, unroll=4)

    def send_inc(i, c):
        j = offset(i)
        send(INC, inc_out.at[j], inc_in.at[tiles - j], line(wrap(z + j)))
        return c

    lax.fori_loop(1, tiles, send_inc, 0)
    inc_in[0] = inc_out[0]

    wait_tiles(w_in, rcv.at[W], 1, tiles - 1)
    cross = jnp.sum(inc_out[...] * w_in[...], axis=0)
    x_out[0] = cross
    to_d = 2 * lax.div(z, 2)
    for half in range(2):
        to = to_d + half

        @pl.when(to != p)
        def _(to=to):
            send(X, x_out.at[0], x_in.at[wrap(p - to)], plane(to))

    @pl.when(owner)
    def _():
        wait_tiles(lz_in, rcv.at[LZ], 1, tiles - 1)
        wait_tiles(x_in, rcv.at[X], 1, tiles - 1)
        r_out[0] = (
            lsum[lax.rem(z, 2)] + jnp.sum(lz_in[1:tiles], axis=0)
            + x_out[0] + jnp.sum(x_in[1:tiles], axis=0)
        )

        def send_r(i, c):
            to = wrap(z + offset(i))
            pltpu.make_async_remote_copy(
                src_ref=r_out.at[0], dst_ref=r_in.at[lax.rem(z, 2)],
                send_sem=snd.at[R], recv_sem=r_rcv.at[lax.rem(z, 2)],
                device_id=line(to), device_id_type=MESH,
            ).start()
            return c

        lax.fori_loop(1, tiles, send_r, 0)

    wait_tiles(inc_in, rcv.at[INC], 1, tiles - 1)

    def finish(i, c):
        cols = pl.ds(pl.multiple_of(i * 256, 256), 256)
        inc = jnp.concatenate([inc_in[wrap(2 * i - z)], inc_in[wrap(2 * i + 1 - z)]], axis=1)
        u = inc * res[:, cols]
        u0 = u.astype(BF16).astype(F32)
        u1 = (u - u0).astype(BF16).astype(F32)
        u2 = u - u0 - u1
        u3 = jnp.concatenate([u0, u1, u2, jnp.zeros_like(u)], axis=0).astype(BF16)
        out = lg[:, cols] + jnp.dot(carry3, u3, preferred_element_type=F32)
        gin_ref[0, :, cols] = out.astype(BF16)
        return c

    lax.fori_loop(0, tiles // 2, finish, 0)

    for i in range(2):
        mine = 2 * d + i == z

        @pl.when(jnp.logical_not(mine))
        def _(i=i):
            wait_tiles(r_in, r_rcv.at[i], i, 1)
            rgrad_ref[:, i * 128:(i + 1) * 128] = r_in[i]

        @pl.when(mine)
        def _(i=i):
            rgrad_ref[:, i * 128:(i + 1) * 128] = r_out[0]

    for kind, buf in ((S, s_in), (W, w_in), (LP, l_in), (INC, inc_in)):
        wait_tiles(buf, snd.at[kind], 1, tiles - 1)
    wait_tiles(tw_in, snd.at[TW], 0, 1)

    for i in range(2):
        @pl.when(2 * d + i != z)
        def _():
            wait_tiles(lsum, snd.at[LZ], 0, 1)

    for half in range(2):
        @pl.when(to_d + half != p)
        def _():
            wait_tiles(x_out, snd.at[X], 0, 1)

    @pl.when(owner)
    def _():
        wait_tiles(s_in, snd.at[R], 1, tiles - 1)


def local(grad_out, block_in, residues, decay_rates):
    _, rows, channels = grad_out.shape
    tiles = channels // 128
    modes = residues.shape[0]
    vm = pltpu.VMEM
    many = vm((tiles, modes, 128), F32)
    one = vm((1, modes, 128), F32)
    pair = vm((2, modes, 128), F32)
    anywhere = pl.BlockSpec(memory_space=pl.ANY)
    shapes = (
        jax.ShapeDtypeStruct((1, rows, channels), BF16),
        jax.ShapeDtypeStruct((modes, 256), F32),
    )
    return pl.pallas_call(
        functools.partial(kernel, tiles),
        out_shape=tuple(vm(a.shape, a.dtype) for a in shapes),
        in_specs=[pl.BlockSpec(memory_space=pltpu.SMEM), anywhere, anywhere, anywhere],
        out_specs=(pl.BlockSpec(memory_space=pltpu.VMEM), pl.BlockSpec(memory_space=pltpu.VMEM)),
        scratch_shapes=[
            vm((rows, channels), BF16),
            vm((rows, channels), BF16),
            vm((modes, channels), F32),
            vm((modes, rows, rows), BF16),
            vm((rows, channels), F32),
            many, many, many, many, many,
            vm((tiles, 2, modes, 128), F32), many, many,
            one, one, one, many, pair, many, one, pair,
            pltpu.SemaphoreType.DMA((3,)),
            pltpu.SemaphoreType.DMA((8,)),
            pltpu.SemaphoreType.DMA((8,)),
            pltpu.SemaphoreType.DMA((2,)),
        ],
        compiler_params=pltpu.CompilerParams(collective_id=0, has_side_effects=True),
        name="modal_backward",
    )(decay_rates, grad_out, block_in, residues)


def solution(mesh):
    placed = (P("dp", "seq", None), P("dp", "seq", None), P(), P())
    return jax.shard_map(
        local,
        mesh=mesh,
        in_specs=placed,
        out_specs=(P("dp", "seq", None), P(None, "dp")),
        check_vma=False,
    )
```

```python
import functools

import jax
import jax.numpy as jnp
from jax import lax
from jax.experimental import pallas as pl
from jax.experimental.pallas import tpu as pltpu
from jax.sharding import PartitionSpec as P

MESH = pl.DeviceIdType.MESH
F32 = jnp.float32
BF16 = jnp.bfloat16


def kernel(
    tiles, cube, rates, g_hbm, x_hbm, res_hbm, gin_ref, rgrad_ref,
    g, x, res, dt, lg, s_out, w_out, l_out, l_in, s1, w1, intra, a_out, a_in, b_out, b_in,
    e_out, e_in, inc_out, inc_in, tw_out, tw_in, x_out, x_in, lsum, lz_in, r_out, r_in,
    in_sem, snd, rcv, r_rcv, far_sem,
):
    modes, rows = 8, 128
    cubes = tiles // cube
    near = tiles // 4
    d = lax.axis_index("dp")
    seq = lax.axis_index("seq")
    h, z = lax.div(seq, tiles), lax.rem(seq, tiles)
    p = 2 * d + h
    e, q = lax.div(z, cube), lax.rem(z, cube)
    tile = q * cubes + e
    owner = lax.div(tile, 2) == d
    S, W, LP, A, B, E, INC, TW, X, LZ, R = range(11)

    def wrap(v, n=tiles):
        return lax.rem(v + n, n)

    def line(zz):
        return (d, h * tiles + zz)

    def plane(pp):
        return (lax.div(pp, 2), lax.rem(pp, 2) * tiles + z)

    def send(kind, src, dst, dev):
        pltpu.make_async_remote_copy(
            src_ref=src, dst_ref=dst, send_sem=snd.at[kind], recv_sem=rcv.at[kind],
            device_id=dev, device_id_type=MESH,
        ).start()

    def wait_tiles(buf, sem, lo, n):
        part = buf.at[pl.ds(lo, n)]
        pltpu.make_async_copy(part, part, sem).wait()

    def got(kind, buf):
        wait_tiles(buf, rcv.at[kind], 1, buf.shape[0] - 1)

    copy_g = pltpu.make_async_copy(g_hbm.at[0], g, in_sem.at[0])
    copy_x = pltpu.make_async_copy(x_hbm.at[0], x, in_sem.at[1])
    copy_r = pltpu.make_async_copy(res_hbm, res, in_sem.at[2])
    copy_g.start()
    copy_x.start()
    copy_r.start()

    barrier = pltpu.get_barrier_semaphore()

    def greet_line(i, c):
        n = near - i
        for to in (wrap(z + n), wrap(z - n)):
            pl.semaphore_signal(barrier, inc=1, device_id=line(to), device_id_type=MESH)
        return c

    def greet_plane(j, c):
        to = plane(wrap(p + j))
        pl.semaphore_signal(barrier, inc=1, device_id=to, device_id_type=MESH)
        return c

    lax.fori_loop(0, near, greet_line, 0)
    lax.fori_loop(1, tiles, greet_plane, 0)

    mode_row = lax.broadcasted_iota(jnp.int32, (modes, 128), 0)
    rate = jnp.zeros((modes, 128), F32)
    for r in range(modes):
        rate = jnp.where(mode_row == r, rates[r], rate)
    gain = jnp.sqrt(1.0 - jnp.exp(-2.0 * rate))
    pos = lax.broadcasted_iota(jnp.int32, (modes, 128), 1).astype(F32)
    state_table = jnp.exp(-rate * pos).astype(BF16)
    carry_t = (gain * jnp.exp(-rate * (rows - pos))).astype(BF16)
    decay = jnp.exp(-rate * float(rows))
    decay_cube = jnp.exp(-rate * float(rows * cube))

    copy_g.wait()
    copy_x.wait()

    def states(i, c):
        cols = pl.ds(pl.multiple_of(i * 256, 256), 256)
        s = jnp.dot(state_table, g[:, cols], preferred_element_type=F32)
        w = jnp.dot(carry_t, x[:, cols], preferred_element_type=F32)
        for t in range(2):
            s_out[2 * i + t] = s[:, t * 128:(t + 1) * 128]
            w_out[2 * i + t] = w[:, t * 128:(t + 1) * 128]
        return c

    lax.fori_loop(0, tiles // 2, states, 0)

    pl.semaphore_wait(barrier, 2 * near + tiles - 1)
    for to in (wrap(z + near), wrap(z - near)):
        pl.semaphore_signal(far_sem, inc=1, device_id=line(to), device_id_type=MESH)

    for kind, src, dst in ((S, s_out, s1), (W, w_out, w1)):
        for n in range(1, cube):
            to = wrap(q + n, cube)
            block = pl.ds(to * cubes, cubes)
            send(kind, src.at[block], dst.at[cube - n], line(e * cube + to))
        dst[0] = src[pl.ds(q * cubes, cubes)]

    lag = (
        lax.broadcasted_iota(jnp.int32, (rows, rows), 1)
        - lax.broadcasted_iota(jnp.int32, (rows, rows), 0)
    ).astype(F32)
    causal = lag >= 0
    lag = jnp.maximum(lag, 0.0)
    for r in range(modes):
        full = jnp.full((rows, rows), rates[r], F32)
        gain_r = jnp.sqrt(1.0 - jnp.exp(-2.0 * full))
        dt[r] = jnp.where(causal, gain_r * jnp.exp(-full * lag), 0.0).astype(BF16)

    copy_r.wait()

    def local(i, c):
        cols = pl.ds(pl.multiple_of(i * 256, 256), 256)
        gc = g[:, cols]
        xc = x[:, cols].astype(F32)
        total = jnp.zeros((rows, 256), F32)
        sums = []
        for r in range(modes):
            v = jnp.dot(dt[r], gc, preferred_element_type=F32)
            total = total + v * res[r:r + 1, cols]
            sums.append(jnp.sum(v * xc, axis=0, keepdims=True))
        lg[:, cols] = total
        lp = jnp.concatenate(sums, axis=0)
        for t in range(2):
            l_out[2 * i + t] = lp[:, t * 128:(t + 1) * 128]
        return c

    lax.fori_loop(0, tiles // 2, local, 0)

    def send_l(j, c):
        to = wrap(p + j)
        pair = pl.ds(2 * lax.div(to, 2), 2)
        send(LP, l_out.at[pair], l_in.at[tiles - j], plane(to))
        return c

    lax.fori_loop(1, tiles, send_l, 0)

    got(S, s1)
    f = jnp.zeros((cubes, modes, 128), F32)
    for j in reversed(range(cube)):
        intra[j] = f
        f = s1[wrap(j - q, cube)] + decay[None] * f
    a_out[...] = f

    pl.semaphore_wait(far_sem, 2)

    def far_first(i):
        m = lax.div(i, 2)
        return cubes // 2 + jnp.where(lax.rem(i, 2) == 0, m, -m)

    def send_a(i, c):
        n = far_first(i)
        to = wrap(e + n, cubes)
        send(A, a_out.at[to], a_in.at[cubes - n], line(to * cube + q))
        return c

    lax.fori_loop(1, cubes, send_a, 0)
    a_in[0] = a_out[e]

    got(W, w1)
    weight = jnp.zeros((cubes, modes, 128), F32)
    cross = jnp.zeros((cubes, modes, 128), F32)
    for j in range(cube):
        wj = w1[wrap(j - q, cube)]
        weight = wj + decay[None] * weight
        cross = cross + intra[j] * wj
    for t in range(cubes):
        b_out[t, 0] = weight[t]
        b_out[t, 1] = cross[t]

    def send_b(i, c):
        n = far_first(i)
        to = wrap(e + n, cubes)
        send(B, b_out.at[to], b_in.at[cubes - n], line(to * cube + q))
        return c

    lax.fori_loop(1, cubes, send_b, 0)
    b_in[0] = b_out[e]

    got(LP, l_in)
    lsum[...] = l_out[pl.ds(2 * d, 2)] + jnp.sum(l_in[1:tiles], axis=0)

    def home(k):
        return lax.rem(k, cubes) * cube + lax.div(k, cubes)

    for i in range(2):
        to = home(2 * d + i)

        @pl.when(to != z)
        def _(i=i, to=to):
            send(LZ, lsum.at[i], lz_in.at[wrap(z - to)], line(to))

    got(A, a_in)

    def scan(f, keep):
        for c in reversed(range(cubes)):
            slot = wrap(c - e, cubes)
            if keep:
                e_out[slot] = f
            f = a_in[slot] + decay_cube * f
        return f

    tw_out[0] = scan(jnp.zeros((modes, 128), F32), False)
    send(TW, tw_out.at[0], tw_in.at[0], plane(p + 1 - 2 * h))
    wait_tiles(tw_in, rcv.at[TW], 0, 1)
    scan(jnp.where(h == 0, tw_in[0], 0.0), True)

    def send_e(i, c):
        n = far_first(i)
        to = wrap(e + n, cubes)
        send(E, e_out.at[n], e_in.at[cubes - n], line(to * cube + q))
        return c

    lax.fori_loop(1, cubes, send_e, 0)
    e_in[0] = e_out[0]

    got(B, b_in)
    total = jnp.zeros((modes, 128), F32)
    for slot in range(cubes):
        total = total + b_in[slot, 1] + e_out[slot] * b_in[slot, 0]
    x_out[0] = total
    to_p = 2 * lax.div(tile, 2)
    for half in range(2):
        to = to_p + half

        @pl.when(to != p)
        def _(to=to):
            send(X, x_out.at[0], x_in.at[wrap(p - to)], plane(to))

    @pl.when(owner)
    def _():
        got(LZ, lz_in)
        got(X, x_in)
        r_out[0] = (
            lsum[lax.rem(tile, 2)] + jnp.sum(lz_in[1:tiles], axis=0)
            + x_out[0] + jnp.sum(x_in[1:tiles], axis=0)
        )

        def send_r(i, c):
            m = lax.div(i, 2)
            n = tiles // 2 + jnp.where(lax.rem(i, 2) == 0, m, -m)
            side = lax.rem(tile, 2)
            pltpu.make_async_remote_copy(
                src_ref=r_out.at[0], dst_ref=r_in.at[side],
                send_sem=snd.at[R], recv_sem=r_rcv.at[side],
                device_id=line(wrap(z + n)), device_id_type=MESH,
            ).start()
            return c

        lax.fori_loop(1, tiles, send_r, 0)

    got(E, e_in)
    for t in range(cubes):
        v = e_in[wrap(t - e, cubes)]
        for j in reversed(range(cube)):
            inc_out[wrap(j - q, cube), t] = intra[j, t] + v
            v = decay * v
    for n in range(1, cube):
        to = wrap(q + n, cube)
        send(INC, inc_out.at[n], inc_in.at[cube - n], line(e * cube + to))
    inc_in[0] = inc_out[0]

    col = lax.rem(lax.broadcasted_iota(jnp.int32, (rows, 32), 1), modes)
    part = lax.div(lax.broadcasted_iota(jnp.int32, (rows, 32), 1), modes)
    at = lax.broadcasted_iota(jnp.int32, (rows, 32), 0).astype(F32)
    rate_c = jnp.zeros((rows, 32), F32)
    for r in range(modes):
        rate_c = jnp.where(col == r, rates[r], rate_c)
    gain_c = jnp.sqrt(1.0 - jnp.exp(-2.0 * rate_c))
    carry3 = jnp.where(part < 3, gain_c * jnp.exp(-rate_c * (rows - at)), 0.0).astype(BF16)

    got(INC, inc_in)

    def finish(i, c):
        cols = pl.ds(pl.multiple_of(i * 256, 256), 256)
        slot = wrap(lax.div(2 * i, cubes) - q, cube)
        t = lax.rem(2 * i, cubes)
        inc = jnp.concatenate([inc_in[slot, t], inc_in[slot, t + 1]], axis=1)
        u = inc * res[:, cols]
        u0 = u.astype(BF16).astype(F32)
        u1 = (u - u0).astype(BF16).astype(F32)
        u2 = u - u0 - u1
        u3 = jnp.concatenate([u0, u1, u2, jnp.zeros_like(u)], axis=0).astype(BF16)
        out = lg[:, cols] + jnp.dot(carry3, u3, preferred_element_type=F32)
        gin_ref[0, :, cols] = out.astype(BF16)
        return c

    lax.fori_loop(0, tiles // 2, finish, 0)

    for i in range(2):
        mine = 2 * d + i == tile

        @pl.when(jnp.logical_not(mine))
        def _(i=i):
            wait_tiles(r_in, r_rcv.at[i], i, 1)
            rgrad_ref[:, i * 128:(i + 1) * 128] = r_in[i]

        @pl.when(mine)
        def _(i=i):
            rgrad_ref[:, i * 128:(i + 1) * 128] = r_out[0]

    drains = ((S, s1), (W, w1), (LP, l_in), (A, a_in), (B, b_in), (E, e_in), (INC, inc_in))
    for kind, buf in drains:
        wait_tiles(buf, snd.at[kind], 1, buf.shape[0] - 1)
    wait_tiles(tw_in, snd.at[TW], 0, 1)
    for i in range(2):
        @pl.when(home(2 * d + i) != z)
        def _():
            wait_tiles(lsum, snd.at[LZ], 0, 1)
    for half in range(2):
        @pl.when(to_p + half != p)
        def _():
            wait_tiles(x_out, snd.at[X], 0, 1)

    @pl.when(owner)
    def _():
        wait_tiles(lz_in, snd.at[R], 1, tiles - 1)


def local(grad_out, block_in, residues, decay_rates):
    _, rows, channels = grad_out.shape
    tiles = channels // 128
    modes = residues.shape[0]
    vm = pltpu.VMEM
    cube = 4 if tiles % 8 == 0 else 2
    cubes = tiles // cube

    def held(*lead):
        return vm((*lead, modes, 128), F32)

    anywhere = pl.BlockSpec(memory_space=pl.ANY)
    shapes = (
        jax.ShapeDtypeStruct((1, rows, channels), BF16),
        jax.ShapeDtypeStruct((modes, 256), F32),
    )
    return pl.pallas_call(
        functools.partial(kernel, tiles, cube),
        out_shape=tuple(vm(a.shape, a.dtype) for a in shapes),
        in_specs=[pl.BlockSpec(memory_space=pltpu.SMEM), anywhere, anywhere, anywhere],
        out_specs=(pl.BlockSpec(memory_space=pltpu.VMEM), pl.BlockSpec(memory_space=pltpu.VMEM)),
        scratch_shapes=[
            vm((rows, channels), BF16),
            vm((rows, channels), BF16),
            vm((modes, channels), F32),
            vm((modes, rows, rows), BF16),
            vm((rows, channels), F32),
            held(tiles), held(tiles), held(tiles), held(tiles, 2),
            held(cube, cubes), held(cube, cubes), held(cube, cubes),
            held(cubes), held(cubes), held(cubes, 2), held(cubes, 2),
            held(cubes), held(cubes), held(cube, cubes), held(cube, cubes),
            held(1), held(1), held(1), held(tiles), held(2), held(tiles), held(1), held(2),
            pltpu.SemaphoreType.DMA((3,)),
            pltpu.SemaphoreType.DMA((11,)),
            pltpu.SemaphoreType.DMA((11,)),
            pltpu.SemaphoreType.DMA((2,)),
            pltpu.SemaphoreType.REGULAR,
        ],
        compiler_params=pltpu.CompilerParams(collective_id=0, has_side_effects=True),
        name="modal_backward",
    )(decay_rates, grad_out, block_in, residues)


def solution(mesh):
    placed = (P("dp", "seq", None), P("dp", "seq", None), P(), P())
    return jax.shard_map(
        local,
        mesh=mesh,
        in_specs=placed,
        out_specs=(P("dp", "seq", None), P(None, "dp")),
        check_vma=False,
    )
```

```python
import functools

import jax
import jax.numpy as jnp
from jax import lax
from jax.experimental import pallas as pl
from jax.experimental.pallas import tpu as pltpu
from jax.sharding import PartitionSpec as P

MESH = pl.DeviceIdType.MESH
F32 = jnp.float32
BF16 = jnp.bfloat16


def kernel(
    tiles, cube, rates, g_hbm, x_hbm, res_hbm, gin_ref, rgrad_ref,
    g, x, res, dt, lg, s_out, w_out, l_out, l_in, s1, w1, intra, a_out, a_in, b_out, b_in,
    e_out, e_in, inc_out, inc_in, tw_out, tw_in, x_out, x_in, lsum, lz_in, r_out, r_in,
    in_sem, snd, rcv, r_rcv, e_rcv, inc_rcv, far_sem,
):
    modes, rows = 8, 128
    cubes = tiles // cube
    near = tiles // 4
    d = lax.axis_index("dp")
    seq = lax.axis_index("seq")
    h, z = lax.div(seq, tiles), lax.rem(seq, tiles)
    p = 2 * d + h
    e, q = lax.div(z, cube), lax.rem(z, cube)
    tile = q * cubes + e
    owner = lax.div(tile, 2) == d
    S, W, LP, A, B, E, INC, TW, X, LZ, R = range(11)

    def wrap(v, n=tiles):
        return lax.rem(v + n, n)

    def line(zz):
        return (d, h * tiles + zz)

    def plane(pp):
        return (lax.div(pp, 2), lax.rem(pp, 2) * tiles + z)

    def send(kind, src, dst, dev):
        pltpu.make_async_remote_copy(
            src_ref=src, dst_ref=dst, send_sem=snd.at[kind], recv_sem=rcv.at[kind],
            device_id=dev, device_id_type=MESH,
        ).start()

    def wait_tiles(buf, sem, lo, n):
        part = buf.at[pl.ds(lo, n)]
        pltpu.make_async_copy(part, part, sem).wait()

    def got(kind, buf):
        wait_tiles(buf, rcv.at[kind], 1, buf.shape[0] - 1)

    copy_g = pltpu.make_async_copy(g_hbm.at[0], g, in_sem.at[0])
    copy_x = pltpu.make_async_copy(x_hbm.at[0], x, in_sem.at[1])
    copy_r = pltpu.make_async_copy(res_hbm, res, in_sem.at[2])
    copy_g.start()
    copy_x.start()
    copy_r.start()

    barrier = pltpu.get_barrier_semaphore()

    def greet_line(i, c):
        n = near - i
        for to in (wrap(z + n), wrap(z - n)):
            pl.semaphore_signal(barrier, inc=1, device_id=line(to), device_id_type=MESH)
        return c

    def greet_plane(j, c):
        to = plane(wrap(p + j))
        pl.semaphore_signal(barrier, inc=1, device_id=to, device_id_type=MESH)
        return c

    lax.fori_loop(0, near, greet_line, 0)
    lax.fori_loop(1, tiles, greet_plane, 0)

    mode_row = lax.broadcasted_iota(jnp.int32, (modes, 128), 0)
    rate = jnp.zeros((modes, 128), F32)
    for r in range(modes):
        rate = jnp.where(mode_row == r, rates[r], rate)
    gain = jnp.sqrt(1.0 - jnp.exp(-2.0 * rate))
    pos = lax.broadcasted_iota(jnp.int32, (modes, 128), 1).astype(F32)
    state_table = jnp.exp(-rate * pos).astype(BF16)
    carry_t = (gain * jnp.exp(-rate * (rows - pos))).astype(BF16)
    decay = jnp.exp(-rate * float(rows))
    decay_cube = jnp.exp(-rate * float(rows * cube))

    copy_g.wait()
    copy_x.wait()

    def states(i, c):
        cols = pl.ds(pl.multiple_of(i * 256, 256), 256)
        s = jnp.dot(state_table, g[:, cols], preferred_element_type=F32)
        w = jnp.dot(carry_t, x[:, cols], preferred_element_type=F32)
        for t in range(2):
            s_out[2 * i + t] = s[:, t * 128:(t + 1) * 128]
            w_out[2 * i + t] = w[:, t * 128:(t + 1) * 128]
        return c

    lax.fori_loop(0, tiles // 2, states, 0)

    pl.semaphore_wait(barrier, 2 * near + tiles - 1)
    for to in (wrap(z + near), wrap(z - near)):
        pl.semaphore_signal(far_sem, inc=1, device_id=line(to), device_id_type=MESH)

    def level_1(kind, src, dst):
        for n in range(1, cube):
            to = wrap(q + n, cube)
            block = pl.ds(to * cubes, cubes)
            send(kind, src.at[block], dst.at[cube - n], line(e * cube + to))
        dst[0] = src[pl.ds(q * cubes, cubes)]

    level_1(S, s_out, s1)

    lag = (
        lax.broadcasted_iota(jnp.int32, (rows, rows), 1)
        - lax.broadcasted_iota(jnp.int32, (rows, rows), 0)
    ).astype(F32)
    causal = lag >= 0
    lag = jnp.maximum(lag, 0.0)
    for r in range(modes):
        full = jnp.full((rows, rows), rates[r], F32)
        gain_r = jnp.sqrt(1.0 - jnp.exp(-2.0 * full))
        dt[r] = jnp.where(causal, gain_r * jnp.exp(-full * lag), 0.0).astype(BF16)

    copy_r.wait()

    def local(i, c):
        cols = pl.ds(pl.multiple_of(i * 256, 256), 256)
        gc = g[:, cols]
        xc = x[:, cols].astype(F32)
        total = jnp.zeros((rows, 256), F32)
        sums = []
        for r in range(modes):
            v = jnp.dot(dt[r], gc, preferred_element_type=F32)
            total = total + v * res[r:r + 1, cols]
            sums.append(jnp.sum(v * xc, axis=0, keepdims=True))
        lg[:, cols] = total
        lp = jnp.concatenate(sums, axis=0)
        for t in range(2):
            l_out[2 * i + t] = lp[:, t * 128:(t + 1) * 128]
        return c

    lax.fori_loop(0, tiles // 4, local, 0)
    level_1(W, w_out, w1)
    lax.fori_loop(tiles // 4, tiles // 2, local, 0)

    got(S, s1)
    f = jnp.zeros((cubes, modes, 128), F32)
    for j in reversed(range(cube)):
        intra[j] = f
        f = s1[wrap(j - q, cube)] + decay[None] * f
    a_out[...] = f

    pl.semaphore_wait(far_sem, 2)

    def far_first(i):
        m = lax.div(i, 2)
        return cubes // 2 + jnp.where(lax.rem(i, 2) == 0, m, -m)

    def send_a(i, c):
        n = far_first(i)
        to = wrap(e + n, cubes)
        send(A, a_out.at[to], a_in.at[cubes - n], line(to * cube + q))
        return c

    lax.fori_loop(1, cubes, send_a, 0)
    a_in[0] = a_out[e]

    got(W, w1)
    weight = jnp.zeros((cubes, modes, 128), F32)
    cross = jnp.zeros((cubes, modes, 128), F32)
    for j in range(cube):
        wj = w1[wrap(j - q, cube)]
        weight = wj + decay[None] * weight
        cross = cross + intra[j] * wj
    b_out[...] = weight

    def send_b(i, c):
        n = far_first(i)
        to = wrap(e + n, cubes)
        send(B, b_out.at[to], b_in.at[cubes - n], line(to * cube + q))
        return c

    lax.fori_loop(1, cubes, send_b, 0)
    b_in[0] = b_out[e]

    mine = pl.ds(q * cubes, cubes)
    l_out[mine] = l_out[mine] + cross

    def send_l(j, c):
        to = wrap(p + j)
        pair = pl.ds(2 * lax.div(to, 2), 2)
        send(LP, l_out.at[pair], l_in.at[tiles - j], plane(to))
        return c

    lax.fori_loop(1, tiles, send_l, 0)

    got(LP, l_in)
    lsum[...] = l_out[pl.ds(2 * d, 2)] + jnp.sum(l_in[1:tiles], axis=0)

    def home(k):
        return lax.rem(k, cubes) * cube + lax.div(k, cubes)

    for i in range(2):
        to = home(2 * d + i)

        @pl.when(to != z)
        def _(i=i, to=to):
            send(LZ, lsum.at[i], lz_in.at[wrap(z - to)], line(to))

    got(A, a_in)

    def scan(f, keep):
        for c in reversed(range(cubes)):
            slot = wrap(c - e, cubes)
            if keep:
                e_out[slot] = f
            f = a_in[slot] + decay_cube * f
        return f

    tw_out[0] = scan(jnp.zeros((modes, 128), F32), False)
    send(TW, tw_out.at[0], tw_in.at[0], plane(p + 1 - 2 * h))
    wait_tiles(tw_in, rcv.at[TW], 0, 1)
    scan(jnp.where(h == 0, tw_in[0], 0.0), True)

    def send_e(i, c):
        n = far_first(i)
        to = wrap(e + n, cubes)
        pltpu.make_async_remote_copy(
            src_ref=e_out.at[n], dst_ref=e_in.at[cubes - n],
            send_sem=snd.at[E], recv_sem=e_rcv.at[cubes - n],
            device_id=line(to * cube + q), device_id_type=MESH,
        ).start()
        return c

    lax.fori_loop(1, cubes, send_e, 0)
    e_in[0] = e_out[0]

    got(B, b_in)
    total = jnp.zeros((modes, 128), F32)
    for slot in range(cubes):
        total = total + e_out[slot] * b_in[slot]
    x_out[0] = total
    to_p = 2 * lax.div(tile, 2)
    for half in range(2):
        to = to_p + half

        @pl.when(to != p)
        def _(to=to):
            send(X, x_out.at[0], x_in.at[wrap(p - to)], plane(to))

    @pl.when(owner)
    def _():
        got(LZ, lz_in)
        got(X, x_in)
        r_out[0] = (
            lsum[lax.rem(tile, 2)] + jnp.sum(lz_in[1:tiles], axis=0)
            + x_out[0] + jnp.sum(x_in[1:tiles], axis=0)
        )

        def send_r(i, c):
            m = lax.div(i, 2)
            n = tiles // 2 + jnp.where(lax.rem(i, 2) == 0, m, -m)
            side = lax.rem(tile, 2)
            pltpu.make_async_remote_copy(
                src_ref=r_out.at[0], dst_ref=r_in.at[side],
                send_sem=snd.at[R], recv_sem=r_rcv.at[side],
                device_id=line(wrap(z + n)), device_id_type=MESH,
            ).start()
            return c

        lax.fori_loop(1, tiles, send_r, 0)

    col = lax.rem(lax.broadcasted_iota(jnp.int32, (rows, 32), 1), modes)
    part = lax.div(lax.broadcasted_iota(jnp.int32, (rows, 32), 1), modes)
    at = lax.broadcasted_iota(jnp.int32, (rows, 32), 0).astype(F32)
    rate_c = jnp.zeros((rows, 32), F32)
    for r in range(modes):
        rate_c = jnp.where(col == r, rates[r], rate_c)
    gain_c = jnp.sqrt(1.0 - jnp.exp(-2.0 * rate_c))
    carry3 = jnp.where(part < 3, gain_c * jnp.exp(-rate_c * (rows - at)), 0.0).astype(BF16)

    order = sorted(range(cubes), key=lambda n: min(n, cubes - n))
    for n in order:
        if n:
            wait_tiles(e_in, e_rcv.at[n], n, 1)
        t = wrap(e + n, cubes)
        v = e_in[n]
        for j in reversed(range(cube)):
            inc_out[n, wrap(j - q, cube)] = intra[j, t] + v
            v = decay * v
        for m in range(1, cube):
            pltpu.make_async_remote_copy(
                src_ref=inc_out.at[n, m], dst_ref=inc_in.at[n, cube - m],
                send_sem=snd.at[INC], recv_sem=inc_rcv.at[n],
                device_id=line(e * cube + wrap(q + m, cube)), device_id_type=MESH,
            ).start()
        inc_in[n, 0] = inc_out[n, 0]

    for n in order:
        wait_tiles(inc_in.at[n], inc_rcv.at[n], 1, cube - 1)
        t = wrap(e + n, cubes)

        def finish(m, c, n=n, t=t):
            k = wrap(q + m, cube) * cubes + t
            cols = pl.ds(pl.multiple_of(k * 128, 128), 128)
            u = inc_in[n, m] * res[:, cols]
            u0 = u.astype(BF16).astype(F32)
            u1 = (u - u0).astype(BF16).astype(F32)
            u2 = u - u0 - u1
            u3 = jnp.concatenate([u0, u1, u2, jnp.zeros_like(u)], axis=0).astype(BF16)
            out = lg[:, cols] + jnp.dot(carry3, u3, preferred_element_type=F32)
            gin_ref[0, :, cols] = out.astype(BF16)
            return c

        lax.fori_loop(0, cube, finish, 0, unroll=2)

    for i in range(2):
        mine = 2 * d + i == tile

        @pl.when(jnp.logical_not(mine))
        def _(i=i):
            wait_tiles(r_in, r_rcv.at[i], i, 1)
            rgrad_ref[:, i * 128:(i + 1) * 128] = r_in[i]

        @pl.when(mine)
        def _(i=i):
            rgrad_ref[:, i * 128:(i + 1) * 128] = r_out[0]

    drains = ((S, s1), (W, w1), (LP, l_in), (A, a_in), (B, b_in), (E, e_in))
    for kind, buf in drains:
        wait_tiles(buf, snd.at[kind], 1, buf.shape[0] - 1)
    wait_tiles(l_in, snd.at[INC], 0, cubes * (cube - 1) // 2)
    wait_tiles(tw_in, snd.at[TW], 0, 1)
    for i in range(2):
        @pl.when(home(2 * d + i) != z)
        def _():
            wait_tiles(lsum, snd.at[LZ], 0, 1)
    for half in range(2):
        @pl.when(to_p + half != p)
        def _():
            wait_tiles(x_out, snd.at[X], 0, 1)

    @pl.when(owner)
    def _():
        wait_tiles(lz_in, snd.at[R], 1, tiles - 1)


def write_out(gin, rgrad, gin_hbm, rgrad_hbm, sem):
    copies = [
        pltpu.make_async_copy(gin, gin_hbm, sem.at[0]),
        pltpu.make_async_copy(rgrad, rgrad_hbm, sem.at[1]),
    ]
    for copy in copies:
        copy.start()
    for copy in copies:
        copy.wait()


def local(grad_out, block_in, residues, decay_rates):
    _, rows, channels = grad_out.shape
    tiles = channels // 128
    modes = residues.shape[0]
    vm = pltpu.VMEM
    cube = 4 if tiles % 8 == 0 else 2
    cubes = tiles // cube

    def held(*lead):
        return vm((*lead, modes, 128), F32)

    anywhere = pl.BlockSpec(memory_space=pl.ANY)
    shapes = (
        jax.ShapeDtypeStruct((1, rows, channels), BF16),
        jax.ShapeDtypeStruct((modes, 256), F32),
    )
    kept = pl.pallas_call(
        functools.partial(kernel, tiles, cube),
        out_shape=tuple(vm(a.shape, a.dtype) for a in shapes),
        in_specs=[pl.BlockSpec(memory_space=pltpu.SMEM), anywhere, anywhere, anywhere],
        out_specs=(pl.BlockSpec(memory_space=pltpu.VMEM), pl.BlockSpec(memory_space=pltpu.VMEM)),
        scratch_shapes=[
            vm((rows, channels), BF16),
            vm((rows, channels), BF16),
            vm((modes, channels), F32),
            vm((modes, rows, rows), BF16),
            vm((rows, channels), F32),
            held(tiles), held(tiles), held(tiles), held(tiles, 2),
            held(cube, cubes), held(cube, cubes), held(cube, cubes),
            held(cubes), held(cubes), held(cubes), held(cubes),
            held(cubes), held(cubes), held(cubes, cube), held(cubes, cube),
            held(1), held(1), held(1), held(tiles), held(2), held(tiles), held(1), held(2),
            pltpu.SemaphoreType.DMA((3,)),
            pltpu.SemaphoreType.DMA((11,)),
            pltpu.SemaphoreType.DMA((11,)),
            pltpu.SemaphoreType.DMA((2,)),
            pltpu.SemaphoreType.DMA((cubes,)),
            pltpu.SemaphoreType.DMA((cubes,)),
            pltpu.SemaphoreType.REGULAR,
        ],
        compiler_params=pltpu.CompilerParams(collective_id=0, has_side_effects=True),
        name="modal_backward",
    )(decay_rates, grad_out, block_in, residues)
    in_vmem = pl.BlockSpec(memory_space=pltpu.VMEM)
    kept = tuple(pltpu.with_memory_space_constraint(a, pltpu.VMEM) for a in kept)
    return pl.pallas_call(
        write_out,
        out_shape=shapes,
        in_specs=[in_vmem, in_vmem],
        out_specs=(anywhere, anywhere),
        scratch_shapes=[pltpu.SemaphoreType.DMA((2,))],
        compiler_params=pltpu.CompilerParams(vmem_limit_bytes=1 << 20),
        name="write_out",
    )(*kept)


def solution(mesh):
    placed = (P("dp", "seq", None), P("dp", "seq", None), P(), P())
    return jax.shard_map(
        local,
        mesh=mesh,
        in_specs=placed,
        out_specs=(P("dp", "seq", None), P(None, "dp")),
        check_vma=False,
    )
```

```python
import functools

import jax
import jax.numpy as jnp
from jax import lax
from jax.experimental import pallas as pl
from jax.experimental.pallas import tpu as pltpu
from jax.sharding import PartitionSpec as P

MESH = pl.DeviceIdType.MESH
F32 = jnp.float32
BF16 = jnp.bfloat16


def kernel(
    tiles, cube, rates, g_hbm, x_hbm, res_hbm, gin_ref, rgrad_ref,
    g, x, res, dt, lg, s_out, w_out, l_out, l_in, s1, w1, intra, a_out, a_in, b_out, b_in,
    e_out, e_in, inc_out, inc_in, tw_out, f_in, x_out, x_in, lsum, lz_in, r_out, r_in,
    in_sem, snd, rcv, r_rcv, e_rcv, inc_rcv, f_rcv, far_sem,
):
    modes, rows = 8, 128
    cubes = tiles // cube
    near = tiles // 4
    d = lax.axis_index("dp")
    seq = lax.axis_index("seq")
    h, z = lax.div(seq, tiles), lax.rem(seq, tiles)
    p = 2 * d + h
    e, q = lax.div(z, cube), lax.rem(z, cube)

    def place(c):
        return c + 2 * lax.div(c, 4) - 4 * lax.div(c, 6)

    tile = q * cubes + place(e)
    owner = lax.div(tile, 2) == d
    S, W, LP, A, B, E, INC, TW, X, LZ, R = range(11)

    def wrap(v, n=tiles):
        return lax.rem(v + n, n)

    def line(zz):
        return (d, h * tiles + zz)

    def plane(pp):
        return (lax.div(pp, 2), lax.rem(pp, 2) * tiles + z)

    def send(kind, src, dst, dev):
        pltpu.make_async_remote_copy(
            src_ref=src, dst_ref=dst, send_sem=snd.at[kind], recv_sem=rcv.at[kind],
            device_id=dev, device_id_type=MESH,
        ).start()

    def wait_tiles(buf, sem, lo, n):
        part = buf.at[pl.ds(lo, n)]
        pltpu.make_async_copy(part, part, sem).wait()

    def got(kind, buf):
        wait_tiles(buf, rcv.at[kind], 1, buf.shape[0] - 1)

    copy_g = pltpu.make_async_copy(g_hbm.at[0], g, in_sem.at[0])
    copy_x = pltpu.make_async_copy(x_hbm.at[0], x, in_sem.at[1])
    copy_r = pltpu.make_async_copy(res_hbm, res, in_sem.at[2])
    copy_g.start()
    copy_x.start()
    copy_r.start()

    barrier = pltpu.get_barrier_semaphore()

    def greet_line(i, c):
        n = near - i
        for to in (wrap(z + n), wrap(z - n)):
            pl.semaphore_signal(barrier, inc=1, device_id=line(to), device_id_type=MESH)
        return c

    def greet_plane(j, c):
        to = plane(wrap(p + j))
        pl.semaphore_signal(barrier, inc=1, device_id=to, device_id_type=MESH)
        return c

    lax.fori_loop(0, near, greet_line, 0)
    lax.fori_loop(1, tiles, greet_plane, 0)

    mode_row = lax.broadcasted_iota(jnp.int32, (modes, 128), 0)
    rate = jnp.zeros((modes, 128), F32)
    for r in range(modes):
        rate = jnp.where(mode_row == r, rates[r], rate)
    gain = jnp.sqrt(1.0 - jnp.exp(-2.0 * rate))
    pos = lax.broadcasted_iota(jnp.int32, (modes, 128), 1).astype(F32)
    state_table = jnp.exp(-rate * pos).astype(BF16)
    carry_t = (gain * jnp.exp(-rate * (rows - pos))).astype(BF16)
    decay = jnp.exp(-rate * float(rows))
    decay_cube = jnp.exp(-rate * float(rows * cube))

    copy_g.wait()
    copy_x.wait()

    def states(i, c):
        cols = pl.ds(pl.multiple_of(i * 256, 256), 256)
        s = jnp.dot(state_table, g[:, cols], preferred_element_type=F32)
        w = jnp.dot(carry_t, x[:, cols], preferred_element_type=F32)
        for t in range(2):
            s_out[2 * i + t] = s[:, t * 128:(t + 1) * 128]
            w_out[2 * i + t] = w[:, t * 128:(t + 1) * 128]
        return c

    lax.fori_loop(0, tiles // 2, states, 0)

    pl.semaphore_wait(barrier, 2 * near + tiles - 1)
    for to in (wrap(z + near), wrap(z - near)):
        pl.semaphore_signal(far_sem, inc=1, device_id=line(to), device_id_type=MESH)

    def level_1(kind, src, dst):
        for n in range(1, cube):
            to = wrap(q + n, cube)
            block = pl.ds(to * cubes, cubes)
            send(kind, src.at[block], dst.at[cube - n], line(e * cube + to))
        dst[0] = src[pl.ds(q * cubes, cubes)]

    level_1(S, s_out, s1)

    lag = (
        lax.broadcasted_iota(jnp.int32, (rows, rows), 1)
        - lax.broadcasted_iota(jnp.int32, (rows, rows), 0)
    ).astype(F32)
    causal = lag >= 0
    lag = jnp.maximum(lag, 0.0)
    for r in range(modes):
        full = jnp.full((rows, rows), rates[r], F32)
        gain_r = jnp.sqrt(1.0 - jnp.exp(-2.0 * full))
        dt[r] = jnp.where(causal, gain_r * jnp.exp(-full * lag), 0.0).astype(BF16)

    copy_r.wait()

    def local(i, c):
        cols = pl.ds(pl.multiple_of(i * 256, 256), 256)
        gc = g[:, cols]
        xc = x[:, cols].astype(F32)
        total = jnp.zeros((rows, 256), F32)
        sums = []
        for r in range(modes):
            v = jnp.dot(dt[r], gc, preferred_element_type=F32)
            total = total + v * res[r:r + 1, cols]
            sums.append(jnp.sum(v * xc, axis=0, keepdims=True))
        lg[:, cols] = total
        lp = jnp.concatenate(sums, axis=0)
        for t in range(2):
            l_out[2 * i + t] = lp[:, t * 128:(t + 1) * 128]
        return c

    lax.fori_loop(0, tiles // 4, local, 0)
    level_1(W, w_out, w1)
    lax.fori_loop(tiles // 4, tiles // 2, local, 0)

    got(S, s1)
    f = jnp.zeros((cubes, modes, 128), F32)
    for j in reversed(range(cube)):
        intra[j] = f
        f = s1[wrap(j - q, cube)] + decay[None] * f
    a_out[...] = f

    def send_a(n):
        to = wrap(e + n, cubes)
        send(A, a_out.at[place(to)], a_in.at[cubes - n], line(to * cube + q))

    def apart(n):
        return cube * min(n, cubes - n)

    by_distance = sorted(range(1, cubes), key=apart, reverse=True)
    for n in by_distance:
        if apart(n) <= near:
            send_a(n)

    pl.semaphore_wait(far_sem, 2)
    for n in by_distance:
        if apart(n) > near:
            send_a(n)
    a_in[0] = a_out[place(e)]

    got(W, w1)
    weight = jnp.zeros((cubes, modes, 128), F32)
    cross = jnp.zeros((cubes, modes, 128), F32)
    for j in range(cube):
        wj = w1[wrap(j - q, cube)]
        weight = wj + decay[None] * weight
        cross = cross + intra[j] * wj
    b_out[...] = weight

    def far_first(i):
        m = lax.div(i, 2)
        return cubes // 2 + jnp.where(lax.rem(i, 2) == 0, m, -m)

    def send_b(i, c):
        n = far_first(i)
        to = wrap(e + n, cubes)
        send(B, b_out.at[place(to)], b_in.at[cubes - n], line(to * cube + q))
        return c

    lax.fori_loop(1, cubes, send_b, 0)
    b_in[0] = b_out[place(e)]

    mine = pl.ds(q * cubes, cubes)
    l_out[mine] = l_out[mine] + cross

    def send_l(j, c):
        to = wrap(p + j)
        pair = pl.ds(2 * lax.div(to, 2), 2)
        send(LP, l_out.at[pair], l_in.at[tiles - j], plane(to))
        return c

    lax.fori_loop(1, tiles, send_l, 0)

    got(LP, l_in)
    lsum[...] = l_out[pl.ds(2 * d, 2)] + jnp.sum(l_in[1:tiles], axis=0)

    def home(k):
        return place(lax.rem(k, cubes)) * cube + lax.div(k, cubes)

    for i in range(2):
        to = home(2 * d + i)

        @pl.when(to != z)
        def _(i=i, to=to):
            send(LZ, lsum.at[i], lz_in.at[wrap(z - to)], line(to))

    got(A, a_in)

    def scan(f, keep):
        for c in reversed(range(cubes)):
            slot = wrap(c - e, cubes)
            if keep:
                e_out[slot] = f
            f = a_in[slot] + decay_cube * f
        return f

    tw_out[0] = scan(jnp.zeros((modes, 128), F32), True)

    @pl.when(h == 1)
    def _():
        f_in[...] = jnp.zeros_like(f_in)

        def send_f(n, c):
            to = wrap(e + n, cubes)
            slot = wrap(-n, cubes)
            pltpu.make_async_remote_copy(
                src_ref=tw_out.at[0], dst_ref=f_in.at[slot],
                send_sem=snd.at[TW], recv_sem=f_rcv.at[slot],
                device_id=(d, to * cube + q), device_id_type=MESH,
            ).start()
            return c

        lax.fori_loop(0, cubes, send_f, 0)

    def send_e(i, c):
        n = far_first(i)
        to = wrap(e + n, cubes)
        pltpu.make_async_remote_copy(
            src_ref=e_out.at[n], dst_ref=e_in.at[cubes - n],
            send_sem=snd.at[E], recv_sem=e_rcv.at[cubes - n],
            device_id=line(to * cube + q), device_id_type=MESH,
        ).start()
        return c

    lax.fori_loop(1, cubes, send_e, 0)
    e_in[0] = e_out[0]

    got(B, b_in)
    total = jnp.zeros((modes, 128), F32)
    for slot in range(cubes):
        total = total + e_out[slot] * b_in[slot]
    reach = jnp.zeros((modes, 128), F32)
    for c in range(cubes):
        reach = b_in[wrap(c - e, cubes)] + decay_cube * reach

    @pl.when(h == 0)
    def _():
        wait_tiles(f_in, f_rcv.at[0], 0, 1)

    total = total + f_in[0] * reach
    x_out[0] = total
    to_p = 2 * lax.div(tile, 2)
    for half in range(2):
        to = to_p + half

        @pl.when(to != p)
        def _(to=to):
            send(X, x_out.at[0], x_in.at[wrap(p - to)], plane(to))

    @pl.when(owner)
    def _():
        got(LZ, lz_in)
        got(X, x_in)
        r_out[0] = (
            lsum[lax.rem(tile, 2)] + jnp.sum(lz_in[1:tiles], axis=0)
            + x_out[0] + jnp.sum(x_in[1:tiles], axis=0)
        )

        def send_r(i, c):
            m = lax.div(i, 2)
            n = tiles // 2 + jnp.where(lax.rem(i, 2) == 0, m, -m)
            side = lax.rem(tile, 2)
            pltpu.make_async_remote_copy(
                src_ref=r_out.at[0], dst_ref=r_in.at[side],
                send_sem=snd.at[R], recv_sem=r_rcv.at[side],
                device_id=line(wrap(z + n)), device_id_type=MESH,
            ).start()
            return c

        lax.fori_loop(1, tiles, send_r, 0)

    col = lax.rem(lax.broadcasted_iota(jnp.int32, (rows, 32), 1), modes)
    part = lax.div(lax.broadcasted_iota(jnp.int32, (rows, 32), 1), modes)
    at = lax.broadcasted_iota(jnp.int32, (rows, 32), 0).astype(F32)
    rate_c = jnp.zeros((rows, 32), F32)
    for r in range(modes):
        rate_c = jnp.where(col == r, rates[r], rate_c)
    gain_c = jnp.sqrt(1.0 - jnp.exp(-2.0 * rate_c))
    carry3 = jnp.where(part < 3, gain_c * jnp.exp(-rate_c * (rows - at)), 0.0).astype(BF16)

    ahead = jnp.exp(-rate * (rows * cube * (cubes - 1 - e)).astype(F32))
    order = sorted(range(cubes), key=lambda n: min(n, cubes - n))
    for n in order:
        if n:
            wait_tiles(e_in, e_rcv.at[n], n, 1)

            @pl.when(h == 0)
            def _(n=n):
                wait_tiles(f_in, f_rcv.at[n], n, 1)

        t = place(wrap(e + n, cubes))
        v = e_in[n] + ahead * f_in[n]
        for j in reversed(range(cube)):
            inc_out[n, wrap(j - q, cube)] = intra[j, t] + v
            v = decay * v
        for m in range(1, cube):
            pltpu.make_async_remote_copy(
                src_ref=inc_out.at[n, m], dst_ref=inc_in.at[n, cube - m],
                send_sem=snd.at[INC], recv_sem=inc_rcv.at[n],
                device_id=line(e * cube + wrap(q + m, cube)), device_id_type=MESH,
            ).start()
        inc_in[n, 0] = inc_out[n, 0]

    for n in order:
        wait_tiles(inc_in.at[n], inc_rcv.at[n], 1, cube - 1)
        t = place(wrap(e + n, cubes))

        def finish(m, c, n=n, t=t):
            k = wrap(q + m, cube) * cubes + t
            cols = pl.ds(pl.multiple_of(k * 128, 128), 128)
            u = inc_in[n, m] * res[:, cols]
            u0 = u.astype(BF16).astype(F32)
            u1 = (u - u0).astype(BF16).astype(F32)
            u2 = u - u0 - u1
            u3 = jnp.concatenate([u0, u1, u2, jnp.zeros_like(u)], axis=0).astype(BF16)
            out = lg[:, cols] + jnp.dot(carry3, u3, preferred_element_type=F32)
            gin_ref[0, :, cols] = out.astype(BF16)
            return c

        lax.fori_loop(0, cube, finish, 0, unroll=2)

    for i in range(2):
        mine = 2 * d + i == tile

        @pl.when(jnp.logical_not(mine))
        def _(i=i):
            wait_tiles(r_in, r_rcv.at[i], i, 1)
            rgrad_ref[:, i * 128:(i + 1) * 128] = r_in[i]

        @pl.when(mine)
        def _(i=i):
            rgrad_ref[:, i * 128:(i + 1) * 128] = r_out[0]

    drains = ((S, s1), (W, w1), (LP, l_in), (A, a_in), (B, b_in), (E, e_in))
    for kind, buf in drains:
        wait_tiles(buf, snd.at[kind], 1, buf.shape[0] - 1)
    wait_tiles(l_in, snd.at[INC], 0, cubes * (cube - 1) // 2)

    @pl.when(h == 1)
    def _():
        wait_tiles(f_in, snd.at[TW], 0, cubes)

    for i in range(2):
        @pl.when(home(2 * d + i) != z)
        def _():
            wait_tiles(lsum, snd.at[LZ], 0, 1)
    for half in range(2):
        @pl.when(to_p + half != p)
        def _():
            wait_tiles(x_out, snd.at[X], 0, 1)

    @pl.when(owner)
    def _():
        wait_tiles(lz_in, snd.at[R], 1, tiles - 1)


def write_out(gin, rgrad, gin_hbm, rgrad_hbm, sem):
    parts = sem.shape[0] - 1
    size = gin.shape[1] // parts
    copies = [pltpu.make_async_copy(rgrad, rgrad_hbm, sem.at[parts])]
    for i in range(parts):
        at = pl.ds(i * size, size)
        copies.append(
            pltpu.make_async_copy(gin.at[0, at], gin_hbm.at[0, at], sem.at[i])
        )
    for copy in copies:
        copy.start()
    for copy in copies:
        copy.wait()


def local(grad_out, block_in, residues, decay_rates):
    _, rows, channels = grad_out.shape
    tiles = channels // 128
    modes = residues.shape[0]
    vm = pltpu.VMEM
    cube = 4 if tiles % 8 == 0 else 2
    cubes = tiles // cube

    def held(*lead):
        return vm((*lead, modes, 128), F32)

    anywhere = pl.BlockSpec(memory_space=pl.ANY)
    shapes = (
        jax.ShapeDtypeStruct((1, rows, channels), BF16),
        jax.ShapeDtypeStruct((modes, 256), F32),
    )
    kept = pl.pallas_call(
        functools.partial(kernel, tiles, cube),
        out_shape=tuple(vm(a.shape, a.dtype) for a in shapes),
        in_specs=[pl.BlockSpec(memory_space=pltpu.SMEM), anywhere, anywhere, anywhere],
        out_specs=(pl.BlockSpec(memory_space=pltpu.VMEM), pl.BlockSpec(memory_space=pltpu.VMEM)),
        scratch_shapes=[
            vm((rows, channels), BF16),
            vm((rows, channels), BF16),
            vm((modes, channels), F32),
            vm((modes, rows, rows), BF16),
            vm((rows, channels), F32),
            held(tiles), held(tiles), held(tiles), held(tiles, 2),
            held(cube, cubes), held(cube, cubes), held(cube, cubes),
            held(cubes), held(cubes), held(cubes), held(cubes),
            held(cubes), held(cubes), held(cubes, cube), held(cubes, cube),
            held(1), held(cubes), held(1), held(tiles), held(2), held(tiles), held(1), held(2),
            pltpu.SemaphoreType.DMA((3,)),
            pltpu.SemaphoreType.DMA((11,)),
            pltpu.SemaphoreType.DMA((11,)),
            pltpu.SemaphoreType.DMA((2,)),
            pltpu.SemaphoreType.DMA((cubes,)),
            pltpu.SemaphoreType.DMA((cubes,)),
            pltpu.SemaphoreType.DMA((cubes,)),
            pltpu.SemaphoreType.REGULAR,
        ],
        compiler_params=pltpu.CompilerParams(collective_id=0, has_side_effects=True),
        name="modal_backward",
    )(decay_rates, grad_out, block_in, residues)
    in_vmem = pl.BlockSpec(memory_space=pltpu.VMEM)
    kept = tuple(pltpu.with_memory_space_constraint(a, pltpu.VMEM) for a in kept)
    return pl.pallas_call(
        write_out,
        out_shape=shapes,
        in_specs=[in_vmem, in_vmem],
        out_specs=(anywhere, anywhere),
        scratch_shapes=[pltpu.SemaphoreType.DMA((9,))],
        compiler_params=pltpu.CompilerParams(vmem_limit_bytes=1 << 20),
        name="write_out",
    )(*kept)


def solution(mesh):
    placed = (P("dp", "seq", None), P("dp", "seq", None), P(), P())
    return jax.shard_map(
        local,
        mesh=mesh,
        in_specs=placed,
        out_specs=(P("dp", "seq", None), P(None, "dp")),
        check_vma=False,
    )
```

```python
import functools

import jax
import jax.numpy as jnp
from jax import lax
from jax.experimental import pallas as pl
from jax.experimental.pallas import tpu as pltpu
from jax.sharding import PartitionSpec as P

MESH = pl.DeviceIdType.MESH
F32 = jnp.float32
BF16 = jnp.bfloat16


def kernel(
    tiles, cube, rates, g_hbm, x_hbm, res_hbm, gin_ref, rgrad_ref,
    g, x, res, dt, lg, s_out, w_out, l_out, l_in, s1, w1, intra, a_out, a_in, b_out, b_in,
    e_out, e_in, inc_out, inc_in, tw_out, f_in, x_out, x_in, lsum, lz_in, r_out, r_in,
    in_sem, snd, rcv, r_rcv, e_rcv, inc_rcv, f_rcv, far_sem,
):
    modes, rows = 8, 128
    cubes = tiles // cube
    near = tiles // 4
    d = lax.axis_index("dp")
    seq = lax.axis_index("seq")
    h, z = lax.div(seq, tiles), lax.rem(seq, tiles)
    p = 2 * d + h
    e, q = lax.div(z, cube), lax.rem(z, cube)

    def place(c):
        return c + 2 * lax.div(c, 4) - 4 * lax.div(c, 6)

    tile = q * cubes + place(e)
    owner = lax.div(tile, 2) == d
    S, W, LP, A, B, E, INC, TW, X, LZ, R = range(11)

    def wrap(v, n=tiles):
        return lax.rem(v + n, n)

    def line(zz):
        return (d, h * tiles + zz)

    def plane(pp):
        return (lax.div(pp, 2), lax.rem(pp, 2) * tiles + z)

    def send(kind, src, dst, dev):
        pltpu.make_async_remote_copy(
            src_ref=src, dst_ref=dst, send_sem=snd.at[kind], recv_sem=rcv.at[kind],
            device_id=dev, device_id_type=MESH,
        ).start()

    def wait_tiles(buf, sem, lo, n):
        part = buf.at[pl.ds(lo, n)]
        pltpu.make_async_copy(part, part, sem).wait()

    def got(kind, buf):
        wait_tiles(buf, rcv.at[kind], 1, buf.shape[0] - 1)

    copy_g = pltpu.make_async_copy(g_hbm.at[0], g, in_sem.at[0])
    copy_x = pltpu.make_async_copy(x_hbm.at[0], x, in_sem.at[1])
    copy_r = pltpu.make_async_copy(res_hbm, res, in_sem.at[2])

    barrier = pltpu.get_barrier_semaphore()

    def greet_line(i, c):
        n = near - i
        for to in (wrap(z + n), wrap(z - n)):
            pl.semaphore_signal(barrier, inc=1, device_id=line(to), device_id_type=MESH)
        return c

    def greet_plane(j, c):
        to = plane(wrap(p + j))
        pl.semaphore_signal(barrier, inc=1, device_id=to, device_id_type=MESH)
        return c

    lax.fori_loop(0, near, greet_line, 0)
    copy_g.start()
    copy_x.start()
    copy_r.start()
    lax.fori_loop(1, tiles, greet_plane, 0)

    mode_row = lax.broadcasted_iota(jnp.int32, (modes, 128), 0)
    rate = jnp.zeros((modes, 128), F32)
    for r in range(modes):
        rate = jnp.where(mode_row == r, rates[r], rate)
    gain = jnp.sqrt(1.0 - jnp.exp(-2.0 * rate))
    pos = lax.broadcasted_iota(jnp.int32, (modes, 128), 1).astype(F32)
    state_table = jnp.exp(-rate * pos).astype(BF16)
    carry_t = (gain * jnp.exp(-rate * (rows - pos))).astype(BF16)
    decay = jnp.exp(-rate * float(rows))
    decay_cube = jnp.exp(-rate * float(rows * cube))

    copy_g.wait()
    copy_x.wait()

    def states(i, c):
        cols = pl.ds(pl.multiple_of(i * 256, 256), 256)
        s = jnp.dot(state_table, g[:, cols], preferred_element_type=F32)
        w = jnp.dot(carry_t, x[:, cols], preferred_element_type=F32)
        for t in range(2):
            s_out[2 * i + t] = s[:, t * 128:(t + 1) * 128]
            w_out[2 * i + t] = w[:, t * 128:(t + 1) * 128]
        return c

    lax.fori_loop(0, tiles // 2, states, 0)

    pl.semaphore_wait(barrier, 2 * near + tiles - 1)
    for to in (wrap(z + near), wrap(z - near)):
        pl.semaphore_signal(far_sem, inc=1, device_id=line(to), device_id_type=MESH)

    def level_1(kind, src, dst):
        for n in range(1, cube):
            to = wrap(q + n, cube)
            block = pl.ds(to * cubes, cubes)
            send(kind, src.at[block], dst.at[cube - n], line(e * cube + to))
        dst[0] = src[pl.ds(q * cubes, cubes)]

    level_1(S, s_out, s1)

    lag = (
        lax.broadcasted_iota(jnp.int32, (rows, rows), 1)
        - lax.broadcasted_iota(jnp.int32, (rows, rows), 0)
    ).astype(F32)
    causal = lag >= 0
    lag = jnp.maximum(lag, 0.0)
    for r in range(modes):
        full = jnp.full((rows, rows), rates[r], F32)
        gain_r = jnp.sqrt(1.0 - jnp.exp(-2.0 * full))
        dt[r] = jnp.where(causal, gain_r * jnp.exp(-full * lag), 0.0).astype(BF16)

    copy_r.wait()

    def local(i, c):
        cols = pl.ds(pl.multiple_of(i * 256, 256), 256)
        gc = g[:, cols]
        xc = x[:, cols].astype(F32)
        total = jnp.zeros((rows, 256), F32)
        sums = []
        for r in range(modes):
            v = jnp.dot(dt[r], gc, preferred_element_type=F32)
            total = total + v * res[r:r + 1, cols]
            sums.append(jnp.sum(v * xc, axis=0, keepdims=True))
        lg[:, cols] = total
        lp = jnp.concatenate(sums, axis=0)
        for t in range(2):
            l_out[2 * i + t] = lp[:, t * 128:(t + 1) * 128]
        return c

    lax.fori_loop(0, tiles // 4, local, 0)
    level_1(W, w_out, w1)
    lax.fori_loop(tiles // 4, tiles // 2, local, 0)

    got(S, s1)
    f = jnp.zeros((cubes, modes, 128), F32)
    for j in reversed(range(cube)):
        intra[j] = f
        f = s1[wrap(j - q, cube)] + decay[None] * f
    a_out[...] = f

    def send_a(n):
        to = wrap(e + n, cubes)
        send(A, a_out.at[place(to)], a_in.at[cubes - n], line(to * cube + q))

    def apart(n):
        return cube * min(n, cubes - n)

    by_distance = sorted(range(1, cubes), key=apart, reverse=True)
    pl.semaphore_wait(far_sem, 2)
    for n in by_distance:
        send_a(n)
    a_in[0] = a_out[place(e)]

    got(W, w1)
    weight = jnp.zeros((cubes, modes, 128), F32)
    cross = jnp.zeros((cubes, modes, 128), F32)
    for j in range(cube):
        wj = w1[wrap(j - q, cube)]
        weight = wj + decay[None] * weight
        cross = cross + intra[j] * wj
    b_out[...] = weight

    def far_first(i):
        m = lax.div(i, 2)
        return cubes // 2 + jnp.where(lax.rem(i, 2) == 0, m, -m)

    def send_b(i, c):
        n = far_first(i)
        to = wrap(e + n, cubes)
        send(B, b_out.at[place(to)], b_in.at[cubes - n], line(to * cube + q))
        return c

    lax.fori_loop(1, cubes, send_b, 0)
    b_in[0] = b_out[place(e)]

    mine = pl.ds(q * cubes, cubes)
    l_out[mine] = l_out[mine] + cross

    def send_l(j, c):
        to = wrap(p + j)
        pair = pl.ds(2 * lax.div(to, 2), 2)
        send(LP, l_out.at[pair], l_in.at[tiles - j], plane(to))
        return c

    lax.fori_loop(1, tiles, send_l, 0)

    got(LP, l_in)
    lsum[...] = l_out[pl.ds(2 * d, 2)] + jnp.sum(l_in[1:tiles], axis=0)

    def home(k):
        return place(lax.rem(k, cubes)) * cube + lax.div(k, cubes)

    for i in range(2):
        to = home(2 * d + i)

        @pl.when(to != z)
        def _(i=i, to=to):
            send(LZ, lsum.at[i], lz_in.at[wrap(z - to)], line(to))

    got(A, a_in)

    def scan(f, keep):
        for c in reversed(range(cubes)):
            slot = wrap(c - e, cubes)
            if keep:
                e_out[slot] = f
            f = a_in[slot] + decay_cube * f
        return f

    tw_out[0] = scan(jnp.zeros((modes, 128), F32), True)

    @pl.when(h == 1)
    def _():
        f_in[...] = jnp.zeros_like(f_in)

        def send_f(n, c):
            to = wrap(e + n, cubes)
            slot = wrap(-n, cubes)
            pltpu.make_async_remote_copy(
                src_ref=tw_out.at[0], dst_ref=f_in.at[slot],
                send_sem=snd.at[TW], recv_sem=f_rcv.at[slot],
                device_id=(d, to * cube + q), device_id_type=MESH,
            ).start()
            return c

        lax.fori_loop(0, cubes, send_f, 0)

    def send_e(i, c):
        n = far_first(i)
        to = wrap(e + n, cubes)
        pltpu.make_async_remote_copy(
            src_ref=e_out.at[n], dst_ref=e_in.at[cubes - n],
            send_sem=snd.at[E], recv_sem=e_rcv.at[cubes - n],
            device_id=line(to * cube + q), device_id_type=MESH,
        ).start()
        return c

    lax.fori_loop(1, cubes, send_e, 0)
    e_in[0] = e_out[0]

    got(B, b_in)
    total = jnp.zeros((modes, 128), F32)
    for slot in range(cubes):
        total = total + e_out[slot] * b_in[slot]
    reach = jnp.zeros((modes, 128), F32)
    for c in range(cubes):
        reach = b_in[wrap(c - e, cubes)] + decay_cube * reach

    @pl.when(h == 0)
    def _():
        wait_tiles(f_in, f_rcv.at[0], 0, 1)

    total = total + f_in[0] * reach
    x_out[0] = total
    to_p = 2 * lax.div(tile, 2)
    for half in range(2):
        to = to_p + half

        @pl.when(to != p)
        def _(to=to):
            send(X, x_out.at[0], x_in.at[wrap(p - to)], plane(to))

    @pl.when(owner)
    def _():
        got(LZ, lz_in)
        got(X, x_in)
        r_out[0] = (
            lsum[lax.rem(tile, 2)] + jnp.sum(lz_in[1:tiles], axis=0)
            + x_out[0] + jnp.sum(x_in[1:tiles], axis=0)
        )

        def send_r(i, c):
            m = lax.div(i, 2)
            n = tiles // 2 + jnp.where(lax.rem(i, 2) == 0, m, -m)
            side = lax.rem(tile, 2)
            pltpu.make_async_remote_copy(
                src_ref=r_out.at[0], dst_ref=r_in.at[side],
                send_sem=snd.at[R], recv_sem=r_rcv.at[side],
                device_id=line(wrap(z + n)), device_id_type=MESH,
            ).start()
            return c

        lax.fori_loop(1, tiles, send_r, 0)

    col = lax.rem(lax.broadcasted_iota(jnp.int32, (rows, 32), 1), modes)
    part = lax.div(lax.broadcasted_iota(jnp.int32, (rows, 32), 1), modes)
    at = lax.broadcasted_iota(jnp.int32, (rows, 32), 0).astype(F32)
    rate_c = jnp.zeros((rows, 32), F32)
    for r in range(modes):
        rate_c = jnp.where(col == r, rates[r], rate_c)
    gain_c = jnp.sqrt(1.0 - jnp.exp(-2.0 * rate_c))
    carry3 = jnp.where(part < 3, gain_c * jnp.exp(-rate_c * (rows - at)), 0.0).astype(BF16)

    ahead = jnp.exp(-rate * (rows * cube * (cubes - 1 - e)).astype(F32))
    order = sorted(range(cubes), key=lambda n: min(n, cubes - n))
    for n in order:
        if n:
            wait_tiles(e_in, e_rcv.at[n], n, 1)

            @pl.when(h == 0)
            def _(n=n):
                wait_tiles(f_in, f_rcv.at[n], n, 1)

        t = place(wrap(e + n, cubes))
        v = e_in[n] + ahead * f_in[n]
        for j in reversed(range(cube)):
            inc_out[n, wrap(j - q, cube)] = intra[j, t] + v
            v = decay * v
        for m in range(1, cube):
            pltpu.make_async_remote_copy(
                src_ref=inc_out.at[n, m], dst_ref=inc_in.at[n, cube - m],
                send_sem=snd.at[INC], recv_sem=inc_rcv.at[n],
                device_id=line(e * cube + wrap(q + m, cube)), device_id_type=MESH,
            ).start()
        inc_in[n, 0] = inc_out[n, 0]

    drains = ((S, s1), (W, w1), (LP, l_in), (A, a_in), (B, b_in), (E, e_in))
    for kind, buf in drains:
        wait_tiles(buf, snd.at[kind], 1, buf.shape[0] - 1)

    @pl.when(h == 1)
    def _():
        wait_tiles(f_in, snd.at[TW], 0, cubes)

    for i in range(2):
        @pl.when(home(2 * d + i) != z)
        def _():
            wait_tiles(lsum, snd.at[LZ], 0, 1)
    for half in range(2):
        @pl.when(to_p + half != p)
        def _():
            wait_tiles(x_out, snd.at[X], 0, 1)

    for n in order:
        wait_tiles(inc_in.at[n], inc_rcv.at[n], 1, cube - 1)
        t = place(wrap(e + n, cubes))

        def finish(m, c, n=n, t=t):
            k = wrap(q + m, cube) * cubes + t
            cols = pl.ds(pl.multiple_of(k * 128, 128), 128)
            u = inc_in[n, m] * res[:, cols]
            u0 = u.astype(BF16).astype(F32)
            u1 = (u - u0).astype(BF16).astype(F32)
            u2 = u - u0 - u1
            u3 = jnp.concatenate([u0, u1, u2, jnp.zeros_like(u)], axis=0).astype(BF16)
            out = lg[:, cols] + jnp.dot(carry3, u3, preferred_element_type=F32)
            gin_ref[0, :, cols] = out.astype(BF16)
            return c

        lax.fori_loop(0, cube, finish, 0, unroll=2)

    wait_tiles(l_in, snd.at[INC], 0, cubes * (cube - 1) // 2)

    @pl.when(owner)
    def _():
        wait_tiles(lz_in, snd.at[R], 1, tiles - 1)

    for i in range(2):
        mine = 2 * d + i == tile

        @pl.when(jnp.logical_not(mine))
        def _(i=i):
            wait_tiles(r_in, r_rcv.at[i], i, 1)
            rgrad_ref[:, i * 128:(i + 1) * 128] = r_in[i]

        @pl.when(mine)
        def _(i=i):
            rgrad_ref[:, i * 128:(i + 1) * 128] = r_out[0]


def write_out(gin, rgrad, gin_hbm, rgrad_hbm, sem):
    parts = sem.shape[0] - 1
    size = gin.shape[1] // parts
    copies = [pltpu.make_async_copy(rgrad, rgrad_hbm, sem.at[parts])]
    for i in range(parts):
        at = pl.ds(i * size, size)
        copies.append(
            pltpu.make_async_copy(gin.at[0, at], gin_hbm.at[0, at], sem.at[i])
        )
    for copy in copies:
        copy.start()
    for copy in copies:
        copy.wait()


def local(grad_out, block_in, residues, decay_rates):
    _, rows, channels = grad_out.shape
    tiles = channels // 128
    modes = residues.shape[0]
    vm = pltpu.VMEM
    cube = 4 if tiles % 8 == 0 else 2
    cubes = tiles // cube

    def held(*lead):
        return vm((*lead, modes, 128), F32)

    anywhere = pl.BlockSpec(memory_space=pl.ANY)
    shapes = (
        jax.ShapeDtypeStruct((1, rows, channels), BF16),
        jax.ShapeDtypeStruct((modes, 256), F32),
    )
    kept = pl.pallas_call(
        functools.partial(kernel, tiles, cube),
        out_shape=tuple(vm(a.shape, a.dtype) for a in shapes),
        in_specs=[pl.BlockSpec(memory_space=pltpu.SMEM), anywhere, anywhere, anywhere],
        out_specs=(pl.BlockSpec(memory_space=pltpu.VMEM), pl.BlockSpec(memory_space=pltpu.VMEM)),
        scratch_shapes=[
            vm((rows, channels), BF16),
            vm((rows, channels), BF16),
            vm((modes, channels), F32),
            vm((modes, rows, rows), BF16),
            vm((rows, channels), F32),
            held(tiles), held(tiles), held(tiles), held(tiles, 2),
            held(cube, cubes), held(cube, cubes), held(cube, cubes),
            held(cubes), held(cubes), held(cubes), held(cubes),
            held(cubes), held(cubes), held(cubes, cube), held(cubes, cube),
            held(1), held(cubes), held(1), held(tiles), held(2), held(tiles), held(1), held(2),
            pltpu.SemaphoreType.DMA((3,)),
            pltpu.SemaphoreType.DMA((11,)),
            pltpu.SemaphoreType.DMA((11,)),
            pltpu.SemaphoreType.DMA((2,)),
            pltpu.SemaphoreType.DMA((cubes,)),
            pltpu.SemaphoreType.DMA((cubes,)),
            pltpu.SemaphoreType.DMA((cubes,)),
            pltpu.SemaphoreType.REGULAR,
        ],
        compiler_params=pltpu.CompilerParams(collective_id=0, has_side_effects=True),
        name="modal_backward",
    )(decay_rates, grad_out, block_in, residues)
    in_vmem = pl.BlockSpec(memory_space=pltpu.VMEM)
    kept = tuple(pltpu.with_memory_space_constraint(a, pltpu.VMEM) for a in kept)
    return pl.pallas_call(
        write_out,
        out_shape=shapes,
        in_specs=[in_vmem, in_vmem],
        out_specs=(anywhere, anywhere),
        scratch_shapes=[pltpu.SemaphoreType.DMA((3,))],
        compiler_params=pltpu.CompilerParams(vmem_limit_bytes=1 << 20),
        name="write_out",
    )(*kept)


def solution(mesh):
    placed = (P("dp", "seq", None), P("dp", "seq", None), P(), P())
    return jax.shard_map(
        local,
        mesh=mesh,
        in_specs=placed,
        out_specs=(P("dp", "seq", None), P(None, "dp")),
        check_vma=False,
    )
```

```python
import functools

import jax
import jax.numpy as jnp
from jax import lax
from jax.experimental import pallas as pl
from jax.experimental.pallas import tpu as pltpu
from jax.sharding import PartitionSpec as P

MESH = pl.DeviceIdType.MESH
F32 = jnp.float32
BF16 = jnp.bfloat16


def kernel(
    tiles, cube, rates, g_hbm, x_hbm, res_hbm, gin_ref, rgrad_ref,
    g, x, res, dt, lg, s_out, w_out, l_out, l_in, s1, w1, intra, a_out, a_in, b_out, b_in,
    e_out, e_in, inc_out, inc_in, tw_out, f_in, x_out, x_in, lsum, lz_in, r_out, r_in,
    in_sem, snd, rcv, r_rcv, e_rcv, inc_rcv, f_rcv, far_sem,
):
    modes, rows = 8, 128
    cubes = tiles // cube
    near = tiles // 4
    d = lax.axis_index("dp")
    seq = lax.axis_index("seq")
    h, z = lax.div(seq, tiles), lax.rem(seq, tiles)
    p = 2 * d + h
    e, q = lax.div(z, cube), lax.rem(z, cube)

    def place(c):
        return c + 2 * lax.div(c, 4) - 4 * lax.div(c, 6)

    tile = q * cubes + place(e)
    owner = lax.div(tile, 2) == d
    S, W, LP, A, B, E, INC, TW, X, LZ, R = range(11)

    def wrap(v, n=tiles):
        return lax.rem(v + n, n)

    def line(zz):
        return (d, h * tiles + zz)

    def plane(pp):
        return (lax.div(pp, 2), lax.rem(pp, 2) * tiles + z)

    def send(kind, src, dst, dev):
        pltpu.make_async_remote_copy(
            src_ref=src, dst_ref=dst, send_sem=snd.at[kind], recv_sem=rcv.at[kind],
            device_id=dev, device_id_type=MESH,
        ).start()

    def wait_tiles(buf, sem, lo, n):
        part = buf.at[pl.ds(lo, n)]
        pltpu.make_async_copy(part, part, sem).wait()

    def got(kind, buf):
        wait_tiles(buf, rcv.at[kind], 1, buf.shape[0] - 1)

    copy_g = pltpu.make_async_copy(g_hbm.at[0], g, in_sem.at[0])
    copy_x = pltpu.make_async_copy(x_hbm.at[0], x, in_sem.at[1])
    copy_r = pltpu.make_async_copy(res_hbm, res, in_sem.at[2])

    barrier = pltpu.get_barrier_semaphore()

    def greet_line(i, c):
        n = near - i
        for to in (wrap(z + n), wrap(z - n)):
            pl.semaphore_signal(barrier, inc=1, device_id=line(to), device_id_type=MESH)
        return c

    def greet_plane(j, c):
        to = plane(wrap(p + j))
        pl.semaphore_signal(barrier, inc=1, device_id=to, device_id_type=MESH)
        return c

    lax.fori_loop(0, near, greet_line, 0)
    copy_g.start()
    copy_x.start()
    copy_r.start()
    lax.fori_loop(1, tiles, greet_plane, 0)

    mode_row = lax.broadcasted_iota(jnp.int32, (modes, 128), 0)
    rate = jnp.zeros((modes, 128), F32)
    for r in range(modes):
        rate = jnp.where(mode_row == r, rates[r], rate)
    gain = jnp.sqrt(1.0 - jnp.exp(-2.0 * rate))
    pos = lax.broadcasted_iota(jnp.int32, (modes, 128), 1).astype(F32)
    state_table = jnp.exp(-rate * pos).astype(BF16)
    carry_t = (gain * jnp.exp(-rate * (rows - pos))).astype(BF16)
    decay = jnp.exp(-rate * float(rows))
    decay_cube = jnp.exp(-rate * float(rows * cube))

    copy_g.wait()
    copy_x.wait()

    def states(i, c):
        cols = pl.ds(pl.multiple_of(i * 256, 256), 256)
        s = jnp.dot(state_table, g[:, cols], preferred_element_type=F32)
        w = jnp.dot(carry_t, x[:, cols], preferred_element_type=F32)
        for t in range(2):
            s_out[2 * i + t] = s[:, t * 128:(t + 1) * 128]
            w_out[2 * i + t] = w[:, t * 128:(t + 1) * 128]
        return c

    lax.fori_loop(0, tiles // 2, states, 0)

    pl.semaphore_wait(barrier, 2 * near + tiles - 1)
    for to in (wrap(z + near), wrap(z - near)):
        pl.semaphore_signal(far_sem, inc=1, device_id=line(to), device_id_type=MESH)

    def level_1(kind, src, dst):
        for n in range(1, cube):
            to = wrap(q + n, cube)
            block = pl.ds(to * cubes, cubes)
            send(kind, src.at[block], dst.at[cube - n], line(e * cube + to))
        dst[0] = src[pl.ds(q * cubes, cubes)]

    level_1(S, s_out, s1)
    level_1(W, w_out, w1)

    lag = (
        lax.broadcasted_iota(jnp.int32, (rows, rows), 1)
        - lax.broadcasted_iota(jnp.int32, (rows, rows), 0)
    ).astype(F32)
    causal = lag >= 0
    lag = jnp.maximum(lag, 0.0)
    for r in range(modes):
        full = jnp.full((rows, rows), rates[r], F32)
        gain_r = jnp.sqrt(1.0 - jnp.exp(-2.0 * full))
        dt[r] = jnp.where(causal, gain_r * jnp.exp(-full * lag), 0.0).astype(BF16)

    copy_r.wait()

    def local(i, c):
        cols = pl.ds(pl.multiple_of(i * 256, 256), 256)
        gc = g[:, cols]
        xc = x[:, cols].astype(F32)
        total = jnp.zeros((rows, 256), F32)
        sums = []
        for r in range(modes):
            v = jnp.dot(dt[r], gc, preferred_element_type=F32)
            total = total + v * res[r:r + 1, cols]
            sums.append(jnp.sum(v * xc, axis=0, keepdims=True))
        lg[:, cols] = total
        lp = jnp.concatenate(sums, axis=0)
        for t in range(2):
            l_out[2 * i + t] = lp[:, t * 128:(t + 1) * 128]
        return c

    lax.fori_loop(0, tiles // 2, local, 0)

    got(S, s1)
    f = jnp.zeros((cubes, modes, 128), F32)
    for j in reversed(range(cube)):
        intra[j] = f
        f = s1[wrap(j - q, cube)] + decay[None] * f
    a_out[...] = f

    def send_a(n):
        to = wrap(e + n, cubes)
        send(A, a_out.at[place(to)], a_in.at[cubes - n], line(to * cube + q))

    def apart(n):
        return cube * min(n, cubes - n)

    by_distance = sorted(range(1, cubes), key=apart, reverse=True)
    pl.semaphore_wait(far_sem, 2)
    for n in by_distance:
        send_a(n)
    a_in[0] = a_out[place(e)]

    got(W, w1)
    weight = jnp.zeros((cubes, modes, 128), F32)
    cross = jnp.zeros((cubes, modes, 128), F32)
    for j in range(cube):
        wj = w1[wrap(j - q, cube)]
        weight = wj + decay[None] * weight
        cross = cross + intra[j] * wj
    mine = pl.ds(q * cubes, cubes)
    l_out[mine] = l_out[mine] + cross

    def send_l(j, c):
        to = wrap(p + j)
        pair = pl.ds(2 * lax.div(to, 2), 2)
        send(LP, l_out.at[pair], l_in.at[tiles - j], plane(to))
        return c

    lax.fori_loop(1, tiles, send_l, 0)

    b_out[...] = weight

    def far_first(i):
        m = lax.div(i, 2)
        return cubes // 2 + jnp.where(lax.rem(i, 2) == 0, m, -m)

    def send_b(i, c):
        n = far_first(i)
        to = wrap(e + n, cubes)
        send(B, b_out.at[place(to)], b_in.at[cubes - n], line(to * cube + q))
        return c

    lax.fori_loop(1, cubes, send_b, 0)
    b_in[0] = b_out[place(e)]

    got(LP, l_in)
    lsum[...] = l_out[pl.ds(2 * d, 2)] + jnp.sum(l_in[1:tiles], axis=0)

    def home(k):
        return place(lax.rem(k, cubes)) * cube + lax.div(k, cubes)

    for i in range(2):
        to = home(2 * d + i)

        @pl.when(to != z)
        def _(i=i, to=to):
            send(LZ, lsum.at[i], lz_in.at[wrap(z - to)], line(to))

    got(A, a_in)

    def scan(f, keep):
        for c in reversed(range(cubes)):
            slot = wrap(c - e, cubes)
            if keep:
                e_out[slot] = f
            f = a_in[slot] + decay_cube * f
        return f

    tw_out[0] = scan(jnp.zeros((modes, 128), F32), True)

    @pl.when(h == 1)
    def _():
        f_in[...] = jnp.zeros_like(f_in)

        def send_f(n, c):
            to = wrap(e + n, cubes)
            slot = wrap(-n, cubes)
            pltpu.make_async_remote_copy(
                src_ref=tw_out.at[0], dst_ref=f_in.at[slot],
                send_sem=snd.at[TW], recv_sem=f_rcv.at[slot],
                device_id=(d, to * cube + q), device_id_type=MESH,
            ).start()
            return c

        lax.fori_loop(0, cubes, send_f, 0)

    def send_e(i, c):
        n = far_first(i)
        to = wrap(e + n, cubes)
        pltpu.make_async_remote_copy(
            src_ref=e_out.at[n], dst_ref=e_in.at[cubes - n],
            send_sem=snd.at[E], recv_sem=e_rcv.at[cubes - n],
            device_id=line(to * cube + q), device_id_type=MESH,
        ).start()
        return c

    lax.fori_loop(1, cubes, send_e, 0)
    e_in[0] = e_out[0]

    got(B, b_in)
    total = jnp.zeros((modes, 128), F32)
    for slot in range(cubes):
        total = total + e_out[slot] * b_in[slot]
    reach = jnp.zeros((modes, 128), F32)
    for c in range(cubes):
        reach = b_in[wrap(c - e, cubes)] + decay_cube * reach

    @pl.when(h == 0)
    def _():
        wait_tiles(f_in, f_rcv.at[0], 0, 1)

    total = total + f_in[0] * reach
    x_out[0] = total
    to_p = 2 * lax.div(tile, 2)
    for half in range(2):
        to = to_p + half

        @pl.when(to != p)
        def _(to=to):
            send(X, x_out.at[0], x_in.at[wrap(p - to)], plane(to))

    @pl.when(owner)
    def _():
        got(LZ, lz_in)
        got(X, x_in)
        r_out[0] = (
            lsum[lax.rem(tile, 2)] + jnp.sum(lz_in[1:tiles], axis=0)
            + x_out[0] + jnp.sum(x_in[1:tiles], axis=0)
        )

        def send_r(i, c):
            m = lax.div(i, 2)
            n = tiles // 2 + jnp.where(lax.rem(i, 2) == 0, m, -m)
            side = lax.rem(tile, 2)
            pltpu.make_async_remote_copy(
                src_ref=r_out.at[0], dst_ref=r_in.at[side],
                send_sem=snd.at[R], recv_sem=r_rcv.at[side],
                device_id=line(wrap(z + n)), device_id_type=MESH,
            ).start()
            return c

        lax.fori_loop(1, tiles, send_r, 0)

    col = lax.rem(lax.broadcasted_iota(jnp.int32, (rows, 32), 1), modes)
    part = lax.div(lax.broadcasted_iota(jnp.int32, (rows, 32), 1), modes)
    at = lax.broadcasted_iota(jnp.int32, (rows, 32), 0).astype(F32)
    rate_c = jnp.zeros((rows, 32), F32)
    for r in range(modes):
        rate_c = jnp.where(col == r, rates[r], rate_c)
    gain_c = jnp.sqrt(1.0 - jnp.exp(-2.0 * rate_c))
    carry3 = jnp.where(part < 3, gain_c * jnp.exp(-rate_c * (rows - at)), 0.0).astype(BF16)

    ahead = jnp.exp(-rate * (rows * cube * (cubes - 1 - e)).astype(F32))
    order = sorted(range(cubes), key=lambda n: min(n, cubes - n))
    for n in order:
        if n:
            wait_tiles(e_in, e_rcv.at[n], n, 1)

            @pl.when(h == 0)
            def _(n=n):
                wait_tiles(f_in, f_rcv.at[n], n, 1)

        t = place(wrap(e + n, cubes))
        v = e_in[n] + ahead * f_in[n]
        for j in reversed(range(cube)):
            inc_out[n, wrap(j - q, cube)] = intra[j, t] + v
            v = decay * v
        for m in range(1, cube):
            pltpu.make_async_remote_copy(
                src_ref=inc_out.at[n, m], dst_ref=inc_in.at[n, cube - m],
                send_sem=snd.at[INC], recv_sem=inc_rcv.at[n],
                device_id=line(e * cube + wrap(q + m, cube)), device_id_type=MESH,
            ).start()
        inc_in[n, 0] = inc_out[n, 0]

    drains = ((S, s1), (W, w1), (LP, l_in), (A, a_in), (B, b_in), (E, e_in))
    for kind, buf in drains:
        wait_tiles(buf, snd.at[kind], 1, buf.shape[0] - 1)

    @pl.when(h == 1)
    def _():
        wait_tiles(f_in, snd.at[TW], 0, cubes)

    for i in range(2):
        @pl.when(home(2 * d + i) != z)
        def _():
            wait_tiles(lsum, snd.at[LZ], 0, 1)
    for half in range(2):
        @pl.when(to_p + half != p)
        def _():
            wait_tiles(x_out, snd.at[X], 0, 1)

    for n in order:
        wait_tiles(inc_in.at[n], inc_rcv.at[n], 1, cube - 1)
        t = place(wrap(e + n, cubes))

        def finish(m, c, n=n, t=t):
            k = wrap(q + m, cube) * cubes + t
            cols = pl.ds(pl.multiple_of(k * 128, 128), 128)
            u = inc_in[n, m] * res[:, cols]
            u0 = u.astype(BF16).astype(F32)
            u1 = (u - u0).astype(BF16).astype(F32)
            u2 = u - u0 - u1
            u3 = jnp.concatenate([u0, u1, u2, jnp.zeros_like(u)], axis=0).astype(BF16)
            out = lg[:, cols] + jnp.dot(carry3, u3, preferred_element_type=F32)
            gin_ref[0, :, cols] = out.astype(BF16)
            return c

        lax.fori_loop(0, cube, finish, 0, unroll=2)

    wait_tiles(l_in, snd.at[INC], 0, cubes * (cube - 1) // 2)

    @pl.when(owner)
    def _():
        wait_tiles(lz_in, snd.at[R], 1, tiles - 1)

    for i in range(2):
        mine = 2 * d + i == tile

        @pl.when(jnp.logical_not(mine))
        def _(i=i):
            wait_tiles(r_in, r_rcv.at[i], i, 1)
            rgrad_ref[:, i * 128:(i + 1) * 128] = r_in[i]

        @pl.when(mine)
        def _(i=i):
            rgrad_ref[:, i * 128:(i + 1) * 128] = r_out[0]


def write_out(gin, rgrad, gin_hbm, rgrad_hbm, sem):
    parts = sem.shape[0] - 1
    size = gin.shape[1] // parts
    copies = [pltpu.make_async_copy(rgrad, rgrad_hbm, sem.at[parts])]
    for i in range(parts):
        at = pl.ds(i * size, size)
        copies.append(
            pltpu.make_async_copy(gin.at[0, at], gin_hbm.at[0, at], sem.at[i])
        )
    for copy in copies:
        copy.start()
    for copy in copies:
        copy.wait()


def local(grad_out, block_in, residues, decay_rates):
    _, rows, channels = grad_out.shape
    tiles = channels // 128
    modes = residues.shape[0]
    vm = pltpu.VMEM
    cube = 4 if tiles % 8 == 0 else 2
    cubes = tiles // cube

    def held(*lead):
        return vm((*lead, modes, 128), F32)

    anywhere = pl.BlockSpec(memory_space=pl.ANY)
    shapes = (
        jax.ShapeDtypeStruct((1, rows, channels), BF16),
        jax.ShapeDtypeStruct((modes, 256), F32),
    )
    kept = pl.pallas_call(
        functools.partial(kernel, tiles, cube),
        out_shape=tuple(vm(a.shape, a.dtype) for a in shapes),
        in_specs=[pl.BlockSpec(memory_space=pltpu.SMEM), anywhere, anywhere, anywhere],
        out_specs=(pl.BlockSpec(memory_space=pltpu.VMEM), pl.BlockSpec(memory_space=pltpu.VMEM)),
        scratch_shapes=[
            vm((rows, channels), BF16),
            vm((rows, channels), BF16),
            vm((modes, channels), F32),
            vm((modes, rows, rows), BF16),
            vm((rows, channels), F32),
            held(tiles), held(tiles), held(tiles), held(tiles, 2),
            held(cube, cubes), held(cube, cubes), held(cube, cubes),
            held(cubes), held(cubes), held(cubes), held(cubes),
            held(cubes), held(cubes), held(cubes, cube), held(cubes, cube),
            held(1), held(cubes), held(1), held(tiles), held(2), held(tiles), held(1), held(2),
            pltpu.SemaphoreType.DMA((3,)),
            pltpu.SemaphoreType.DMA((11,)),
            pltpu.SemaphoreType.DMA((11,)),
            pltpu.SemaphoreType.DMA((2,)),
            pltpu.SemaphoreType.DMA((cubes,)),
            pltpu.SemaphoreType.DMA((cubes,)),
            pltpu.SemaphoreType.DMA((cubes,)),
            pltpu.SemaphoreType.REGULAR,
        ],
        compiler_params=pltpu.CompilerParams(collective_id=0, has_side_effects=True),
        name="modal_backward",
    )(decay_rates, grad_out, block_in, residues)
    in_vmem = pl.BlockSpec(memory_space=pltpu.VMEM)
    kept = tuple(pltpu.with_memory_space_constraint(a, pltpu.VMEM) for a in kept)
    return pl.pallas_call(
        write_out,
        out_shape=shapes,
        in_specs=[in_vmem, in_vmem],
        out_specs=(anywhere, anywhere),
        scratch_shapes=[pltpu.SemaphoreType.DMA((3,))],
        compiler_params=pltpu.CompilerParams(vmem_limit_bytes=1 << 20),
        name="write_out",
    )(*kept)


def solution(mesh):
    placed = (P("dp", "seq", None), P("dp", "seq", None), P(), P())
    return jax.shard_map(
        local,
        mesh=mesh,
        in_specs=placed,
        out_specs=(P("dp", "seq", None), P(None, "dp")),
        check_vma=False,
    )
```
